32 devices in a mesh: shard: 8 (over y, x, core), group: 4 (over z).
Axes of the slice: x: 2, y: 2, z: 4, core: 2. Of those that a mesh axis runs over, the one named last changes fastest.
Arguments:
- layer_input_rows: bfloat16 [32768, 1472], P(('shard', 'group')), may hold values from -6 to 6
- gain_attn: bfloat16 [1472], P('group'), may hold values from 0.5 to 1.5
- w_query: bfloat16 [1472, 384], P('group'), may hold values from -0.0390625 to 0.0390625
- w_key: bfloat16 [1472, 384], P('group'), may hold values from -0.15625 to 0.15625
- w_value: bfloat16 [1472, 384], P('group'), may hold values from -0.15625 to 0.15625
- w_out: bfloat16 [384, 1472], P('group'), may hold values from -1.75 to 1.75
- gain_ff: bfloat16 [1472], P('group'), may hold values from 0.5 to 1.5
- gate_weight: bfloat16 [1472, 3584], P('group'), may hold values from -0.15625 to 0.15625
- w_up: bfloat16 [1472, 3584], P('group'), may hold values from -0.15625 to 0.15625
- w_down: bfloat16 [3584, 1472], P('group'), may hold values from -0.09375 to 0.09375
- bucket_head_bias: bfloat16 [32, 6], P('group'), may hold values from -4 to 4
- positions: int32 [32768], P(('shard', 'group')), may hold values from 0 to 766, as said below
- rel_bucket: int32 [1024], replicated, may hold values from 0 to 31, as said below
- out_grad: bfloat16 [32768, 1472], P(('shard', 'group')), may hold values from -6 to 6
Outputs:
- block_output: bfloat16 [32768, 1472], P(('shard', 'group'))
- input_grad: bfloat16 [32768, 1472], P(('shard', 'group'))
- grad_gain_attn: float32 [1472], P('group')
- grad_query: float32 [1472, 384], P('group')
- grad_key: float32 [1472, 384], P('group')
- grad_value: float32 [1472, 384], P('group')
- grad_out_proj: float32 [384, 1472], P('group')
- grad_gain_ff: float32 [1472], P('group')
- grad_gate: float32 [1472, 3584], P('group')
- grad_up: float32 [1472, 3584], P('group')
- grad_down: float32 [3584, 1472], P('group')
- grad_bias_table: float32 [32, 6], P('group')
The draws below stay inside these ranges and needn't reach their ends.
Inputs may be any that keep to these rules, and one draw needn't show every extreme that they name: Each run of 512 tokens is one sequence whose positions rise by one from a start of 0 to 255; some sequence starts at 0 and some at 255. `rel_bucket`: entry r + 512 is the bucket of relative distance r (key minus query position): 0 at r = 0, not falling with |r|, 16 or more exactly where r > 0.
All inputs are finite; a program needn't handle non-finite values.
Results may differ from the reference program's by a relative error of at most 0.019.
Values may be sent and summed in bfloat16 or wider, within the bound.
No kernel may reach another device: no remote copies, remote signals or barrier semaphores. Data moves between devices by JAX's collectives and lax.ppermute only.
A program may use at most 320 MiB of HBM per device.

```python
import math
import jax
import jax.numpy as jnp
from jax import lax

D = 1472
H = 6
DK = 64
FF = 3584
BUCKETS = 32
SEQ = 512
BLOCK = 256
TOKENS = 32768


def draw_positions(key, part):
    sequences = TOKENS // SEQ
    starts = jax.random.randint(key, (sequences,), 0, BLOCK, dtype=jnp.int32)
    starts = starts.at[0].set(BLOCK - 1).at[sequences - 1].set(0)
    return (starts[:, None] + jnp.arange(SEQ, dtype=jnp.int32)[None, :]).reshape(-1)


def draw_rel_bucket(key, part):
    range_limits = jnp.array([11, 16, 23, 32, 45, 64, 91], dtype=jnp.int32) + jax.random.randint(key, (7,), -2, 3, dtype=jnp.int32)
    distance = jnp.arange(2 * SEQ, dtype=jnp.int32) - SEQ
    magnitude = jnp.abs(distance)
    coarse = 8 + jnp.sum((magnitude[:, None] >= range_limits[None, :]).astype(jnp.int32), axis=1)
    return (jnp.where(magnitude < 8, magnitude, coarse) + jnp.where(distance > 0, 16, 0)).astype(jnp.int32)


def strengthened(values, key, source, target, blocks, factor):
    owner, partner = [(jnp.arange(values.shape[axis_at]) // (values.shape[axis_at] // blocks)).reshape([-1 if axis == axis_at else 1 for axis in range(values.ndim)]) for axis_at in (source, target)]
    chosen = jax.random.permutation(key, blocks)[partner]
    strong = (owner == chosen) | (owner == (partner + blocks // 2) % blocks)
    return jnp.where(strong, factor * values, values)


def block_scale(own_key, extent, cuts, smallest, largest):
    factor_of = 1.0
    for position, shards_of in cuts:
        heights = jax.random.uniform(jax.random.fold_in(jax.random.fold_in(own_key, 6), position), (shards_of,), jnp.float32, smallest / len(cuts), largest / len(cuts))
        factor_of = factor_of * jnp.repeat(jnp.exp(heights), extent[position] // shards_of).reshape((-1,) + (1,) * (len(extent) - 1 - position))
    return factor_of


def centred(rng, extent, scale, reach, cuts=(), kind=jnp.bfloat16):
    values = scale * jax.random.normal(rng, extent, jnp.float32)
    if cuts:
        values = values * block_scale(rng, extent, cuts, -0.22, 0.18)
    return jnp.clip(values, -reach, reach).astype(kind)


def heavy_noise(own_key, extent, scale, reach, pieces, heavy, kind=jnp.bfloat16):
    entries = scale * jax.random.normal(own_key, extent, jnp.float32)
    if pieces:
        entries = entries * block_scale(own_key, extent, pieces, -0.22, 0.18)
    return jnp.clip(strengthened(entries, jax.random.fold_in(own_key, 3), *heavy), -reach, reach).astype(kind)


def setup_inputs(seed: int = 0) -> dict:
    key_of = jax.random.split(jax.random.key(seed), 15)
    return {
        "layer_input_rows": centred(key_of[0], (TOKENS, D), 1.0, 6.0, ((0, 32),)),
        "gain_attn": jnp.clip(1.0 + 0.1 * jax.random.normal(key_of[1], (D,), jnp.float32), 0.5, 1.5).astype(jnp.bfloat16),
        "w_query": centred(key_of[2], (D, H * DK), (16 * D) ** -0.5, 0.0390625, ((0, 4),)),
        "w_key": centred(key_of[3], (D, H * DK), D ** -0.5, 0.15625, ((0, 4),)),
        "w_value": centred(key_of[4], (D, H * DK), D ** -0.5, 0.15625, ((0, 4),)),
        "w_out": centred(key_of[5], (H * DK, D), (H * DK // 32) ** -0.5, 1.75, ((0, 4),)),
        "gain_ff": jnp.clip(1.0 + 0.1 * jax.random.normal(key_of[6], (D,), jnp.float32), 0.5, 1.5).astype(jnp.bfloat16),
        "gate_weight": centred(key_of[7], (D, FF), D ** -0.5, 0.15625, ((0, 4),)),
        "w_up": centred(key_of[8], (D, FF), D ** -0.5, 0.15625, ((0, 4),)),
        "w_down": centred(key_of[9], (FF, D), FF ** -0.5, 0.09375, ((0, 4),)),
        "bucket_head_bias": centred(key_of[10], (BUCKETS, H), 1.0, 4.0, ((0, 4),)),
        "positions": draw_positions(jax.random.fold_in(key_of[14], 71), 0),
        "rel_bucket": draw_rel_bucket(jax.random.fold_in(key_of[14], 71), 0),
        "out_grad": heavy_noise(key_of[13], (TOKENS, D), 1.0, 6.0, ((0, 32),), (0, 1, 32, 2.75)),
    }


@jax.custom_vjp
def low(v):
    return lax.optimization_barrier(v.astype(jnp.bfloat16)).astype(jnp.float32)

@jax.custom_vjp
def low_back(v):
    return v

def low_keep(v):
    return (low(v), None)

def low_pass(kept, grad):
    return (grad,)

def back_keep(v):
    return (v, None)

def back_low(kept, grad):
    return (low(grad),)
low.defvjp(low_keep, low_pass)
low_back.defvjp(back_keep, back_low)
stability_floor = 1e-06

def rounded(values):
    return low_back(low(values))

def normalize(values, gain_vec):
    return values * lax.rsqrt(lax.optimization_barrier(jnp.mean(values * values, axis=-1, keepdims=True)) + stability_floor) * gain_vec

def project(left_bound, right_bound):
    return jnp.einsum('rux,xb->rub', left_bound, right_bound, precision=lax.Precision.HIGHEST)

def forward(params, inputs, places, rel_bucket):
    gain_attn, w_query, w_key, w_value, w_out, gain_ff, gate_weight, w_up, w_down, bucket_head_bias = params
    batch_seqs = inputs.shape[0]
    normed = low(normalize(inputs, gain_attn))
    query_heads = rounded(project(normed, w_query)).reshape(batch_seqs, SEQ, H, DK)
    key_heads = rounded(project(normed, w_key)).reshape(batch_seqs, SEQ, H, DK)
    value_heads = rounded(project(normed, w_value)).reshape(batch_seqs, SEQ, H, DK)
    offsets = jnp.take(bucket_head_bias, rel_bucket, axis=0)
    relative = places[:, None, :] - places[:, :, None] + SEQ
    bias_full = jnp.moveaxis(jnp.take(offsets, relative, axis=0), 3, 1)
    scores = low_back(jnp.einsum('sihd,sjhd->shij', query_heads, key_heads, precision=lax.Precision.HIGHEST) + bias_full)
    blocks = places // BLOCK
    allowed = (blocks[:, None, :] <= blocks[:, :, None])[:, None, :, :]
    attend = jax.nn.softmax(jnp.where(allowed, scores, -1e+30), axis=-1)
    context = rounded(jnp.einsum('shij,sjhd->sihd', low(attend), value_heads, precision=lax.Precision.HIGHEST))
    context = context.reshape(batch_seqs, SEQ, H * DK)
    middle = inputs + low_back(project(context, w_out))
    normed_ff = low(normalize(middle, gain_ff))
    gate_val = rounded(project(normed_ff, gate_weight))
    up_val = rounded(project(normed_ff, w_up))
    hidden = low(jax.nn.gelu(gate_val, approximate=True) * up_val)
    return middle + low_back(project(hidden, w_down))

def reference(layer_input_rows, gain_attn, w_query, w_key, w_value, w_out, gain_ff, gate_weight, w_up, w_down, bucket_head_bias, positions, rel_bucket, out_grad):
    params = tuple((weight.astype(jnp.float32) for weight in (gain_attn, w_query, w_key, w_value, w_out, gain_ff, gate_weight, w_up, w_down, bucket_head_bias)))
    seq_total = layer_input_rows.shape[0] // SEQ
    per_step = math.gcd(max(1, 4096 // SEQ), seq_total)
    steps_count = seq_total // per_step
    inputs = layer_input_rows.astype(jnp.float32).reshape(steps_count, per_step, SEQ, D)
    places = positions.reshape(steps_count, per_step, SEQ)
    cotangent = out_grad.astype(jnp.float32).reshape(steps_count, per_step, SEQ, D)

    def scan_step(totals, element):
        inputs_now, places_now, cotangent_now = element

        def layer_fn(params_now, inputs_in):
            return forward(params_now, inputs_in, places_now, rel_bucket)
        output, pullback = jax.vjp(layer_fn, params, inputs_now)
        grads_now, input_now = pullback(cotangent_now)
        totals = tuple((left_bound + right_bound for left_bound, right_bound in zip(totals, grads_now)))
        return (totals, (output.astype(jnp.bfloat16), input_now.astype(jnp.bfloat16)))
    initial = tuple((jnp.zeros_like(weight) for weight in params))
    totals, (outputs, input_grads) = lax.scan(scan_step, initial, (inputs, places, cotangent))
    return (outputs.reshape(-1, D), input_grads.reshape(-1, D), totals[0], totals[1], totals[2], totals[3], totals[4], totals[5], totals[6], totals[7], totals[8], totals[9])
```

```python
import functools

import jax
import jax.numpy as jnp
from jax import lax
from jax.experimental import pallas as pl
from jax.experimental.pallas import tpu as pltpu
from jax.sharding import PartitionSpec as P

H = 6
DK = 64
SEQ = 512
BLOCK = 256
FLOOR = 1e-06
ROOT = 0.7978845608028654
CUBIC = 0.044715
RB = 128
MB = 512
VMEM_LIMIT = 60 << 20
NT = (((1,), (1,)), ((), ()))
TN = (((0,), (0,)), ((), ()))
ANY = pl.BlockSpec(memory_space=pl.ANY)
bf16 = jnp.bfloat16
f32 = jnp.float32
CORE, XBIT, YBIT = 1, 2, 4


def kernel_cost(us):
    return pl.CostEstimate(flops=int(us * 1.15e9), bytes_accessed=int(us * 1e6), transcendentals=0)


def skew_bias(off_ref, bias_ref):
    rows = jnp.broadcast_to(off_ref[0], (SEQ, 2 * SEQ))
    bias_ref[0] = pltpu.roll(rows, SEQ, 1, stride=1, stride_axis=0)[:, :SEQ].astype(bias_ref.dtype)


def bias_matrix(offsets):
    return pl.pallas_call(
        skew_bias,
        grid=(H,),
        in_specs=[pl.BlockSpec((1, 1, 2 * SEQ), lambda h: (h, 0, 0))],
        out_specs=pl.BlockSpec((1, SEQ, SEQ), lambda h: (h, 0, 0)),
        out_shape=jax.ShapeDtypeStruct((H, SEQ, SEQ), bf16),
        cost_estimate=kernel_cost(4),
        name="bias_matrix",
    )(offsets)


def half_lanes(v, side):
    lane = lax.broadcasted_iota(jnp.int32, v.shape, 1)
    return jnp.where((lane < DK) == (side == 0), v, jnp.zeros_like(v))


def attend_kernel(q_ref, k_ref, v_ref, bias_ref, row_ref, col_ref, attend_ref, ctx_ref):
    keys = k_ref[...]
    values = v_ref[...]
    col = col_ref[0]
    for b in range(SEQ // RB):
        rows = pl.ds(b * RB, RB)
        allowed = col <= row_ref[0, rows]
        ctx = None
        for side in range(2):
            s = lax.dot_general(half_lanes(q_ref[rows], side), keys, NT, preferred_element_type=f32)
            s = jnp.where(allowed, s + bias_ref[side, rows].astype(f32), -1e30)
            p = jnp.exp(s - jnp.max(s, axis=-1, keepdims=True))
            p = (p * (1.0 / jnp.sum(p, axis=-1, keepdims=True))).astype(bf16)
            attend_ref[0, side, rows] = p
            part = half_lanes(jnp.dot(p, values, preferred_element_type=f32), side)
            ctx = part if ctx is None else ctx + part
        ctx_ref[rows] = ctx.astype(bf16)


def pair(which):
    return pl.BlockSpec((SEQ, 2 * DK), lambda h, s: (s, which * (H // 2) + h))


def attend_forward(qkv, bias, row, col):
    n = qkv.shape[0] // SEQ
    return pl.pallas_call(
        attend_kernel,
        grid=(H // 2, n),
        in_specs=[
            pair(0),
            pair(1),
            pair(2),
            pl.BlockSpec((2, SEQ, SEQ), lambda h, s: (h, 0, 0)),
            pl.BlockSpec((1, SEQ, 1), lambda h, s: (s, 0, 0)),
            pl.BlockSpec((1, 1, SEQ), lambda h, s: (s, 0, 0)),
        ],
        out_specs=[pl.BlockSpec((1, 2, SEQ, SEQ), lambda h, s: (s, h, 0, 0)), pair(0)],
        out_shape=[jax.ShapeDtypeStruct((n, H, SEQ, SEQ), bf16), jax.ShapeDtypeStruct((n * SEQ, H * DK), bf16)],
        cost_estimate=kernel_cost(20),
        name="attend_forward",
    )(qkv, qkv, qkv, bias, row, col)


def attend_back_kernel(q_ref, k_ref, v_ref, attend_ref, dctx_ref, dq_ref, dk_ref, dv_ref, skew_ref, ds_ref, skew_sum):
    keys = k_ref[...]
    values = v_ref[...]

    @pl.when(pl.program_id(1) == 0)
    def _():
        skew_sum[...] = jnp.zeros_like(skew_sum)

    for b in range(SEQ // RB):
        rows = pl.ds(b * RB, RB)
        start = SEQ - RB * b
        dq = None
        for side in range(2):
            p = attend_ref[0, side, rows].astype(f32)
            da = lax.dot_general(half_lanes(dctx_ref[rows], side), values, NT, preferred_element_type=f32)
            ds = (p * (da - jnp.sum(p * da, axis=-1, keepdims=True))).astype(bf16)
            ds_ref[side, rows] = ds
            part = half_lanes(jnp.dot(ds, keys, preferred_element_type=f32), side)
            dq = part if dq is None else dq + part
            skew_sum[side, :, start : start + SEQ] += ds.astype(f32)
        dq_ref[rows] = dq.astype(bf16)
    dk, dv = None, None
    for side in range(2):
        part = half_lanes(lax.dot_general(ds_ref[side], q_ref[...], TN, preferred_element_type=f32), side)
        dk = part if dk is None else dk + part
        part = half_lanes(lax.dot_general(attend_ref[0, side], dctx_ref[...], TN, preferred_element_type=f32), side)
        dv = part if dv is None else dv + part
    dk_ref[...] = dk.astype(bf16)
    dv_ref[...] = dv.astype(bf16)

    @pl.when(pl.program_id(1) == pl.num_programs(1) - 1)
    def _():
        for side in range(2):
            total = skew_sum[side, 0:8]
            for u in range(1, RB // 8):
                total += pltpu.roll(skew_sum[side, 8 * u : 8 * u + 8], 2 * SEQ - 8 * u, 1)
            row = lax.broadcasted_iota(jnp.int32, total.shape, 0)
            for bit in (1, 2, 4):
                total = jnp.where((row & bit) != 0, pltpu.roll(total, 2 * SEQ - bit, 1), total)
            skew_ref[side] = jnp.sum(total, axis=0, keepdims=True)


def attend_backward(qkv, attend, dctx):
    n = qkv.shape[0] // SEQ
    out = jax.ShapeDtypeStruct(dctx.shape, bf16)
    return pl.pallas_call(
        attend_back_kernel,
        grid=(H // 2, n),
        in_specs=[pair(0), pair(1), pair(2), pl.BlockSpec((1, 2, SEQ, SEQ), lambda h, s: (s, h, 0, 0)), pair(0)],
        out_specs=[pair(0), pair(0), pair(0), pl.BlockSpec((2, 1, 2 * SEQ), lambda h, s: (h, 0, 0))],
        out_shape=[out, out, out, jax.ShapeDtypeStruct((H, 1, 2 * SEQ), f32)],
        scratch_shapes=[pltpu.VMEM((2, SEQ, SEQ), bf16), pltpu.VMEM((2, RB, 2 * SEQ), f32)],
        cost_estimate=kernel_cost(22),
        name="attend_backward",
    )(qkv, qkv, qkv, attend, dctx)


class Copies:
    def __init__(self, sems):
        self.sems = sems; self.count = 0
    def start(self, src, dst):
        copy = pltpu.make_async_copy(src, dst, self.sems.at[self.count])
        self.count += 1
        copy.start()
        return copy

def wait(copies):
    for c in copies: c.wait()

def load_gate_up(copies, scal, wgu, own_gate, own_up, mine, other, groups):
    z, chunk, core = scal[0], scal[1], scal[2]
    block = own_gate.shape[1]
    started = []
    if other is None:
        for side in range(2):
            for at in range(groups):
                started.append(copies.start(mine.at[side, at], wgu.at[side, at * block : (at + 1) * block]))
        return started
    here = pl.ds(pl.multiple_of(z * block, 16), block)
    started.append(copies.start(own_gate.at[chunk], wgu.at[0, here]))
    started.append(copies.start(own_up.at[chunk], wgu.at[1, here]))
    for k in range(1, groups):
        at = lax.rem(z - k + groups, groups) * block
        for parts, side in ((mine, core), (other, 1 - core)):
            base = 0
            for part in parts:
                n = part.shape[1]
                started.append(copies.start(part.at[k - 1], wgu.at[side, pl.ds(pl.multiple_of(at + base, 8), n)]))
                base += n
    return started

def load_down(copies, scal, wd, own_down, mine, other, groups):
    z, chunk, core = scal[0], scal[1], scal[2]
    block = own_down.shape[1]
    if other is None:
        started = []
        half = block // 2
        for side in range(2):
            for at in range(groups):
                base = at * block + side * half
                started.append(copies.start(mine.at[side, at], wd.at[base : base + half]))
        return started
    started = [copies.start(own_down.at[chunk], wd.at[pl.ds(pl.multiple_of(z * block, 8), block)])]
    for k in range(1, groups):
        at = lax.rem(z - k + groups, groups) * block
        for parts, side in ((mine, core), (other, 1 - core)):
            base = at + side * (block // 2)
            for part in parts:
                n = part.shape[1]
                started.append(copies.start(part.at[k - 1], wd.at[pl.ds(pl.multiple_of(base, 8), n)]))
                base = base + n
    return started

def take_parts(it, n):
    if n == 0:
        return next(it), None
    return [next(it) for _ in range(n)], [next(it) for _ in range(n)]


def parts_of(source):
    if not isinstance(source, tuple):
        return 0, [source], source.shape[0] * source.shape[1]
    mine, other = source
    return len(mine), [*mine, *other], 2 + 2 * len(mine) * mine[0].shape[0]


def ffn_kernel(groups, nparts, *refs):
    it = iter(refs)
    scal = next(it); x_h, xt_h, g_h, own_gate, own_up, own_down = [next(it) for _ in range(6)]
    mine, other = take_parts(it, nparts[0])
    mine_d, other_d = take_parts(it, nparts[1])
    hid_h, dg_h, du_h, gm_h, go_h, gdm_h, gdo_h = [next(it) for _ in range(7)]
    x, xt, g, wgu, wd, hid, dga, dup, hidt, ggu, gd, sems = [next(it) for _ in range(12)]
    copies = Copies(sems)
    core = scal[2]
    c_x = copies.start(x_h, x)
    c_gu = load_gate_up(copies, scal, wgu, own_gate, own_up, mine, other, groups)
    c_g = copies.start(g_h, g)
    c_d = load_down(copies, scal, wd, own_down, mine_d, other_d, groups)
    c_xt = copies.start(xt_h, xt)
    c_x.wait(); wait(c_gu); c_g.wait(); wait(c_d)
    tokens = x.shape[0]
    mb = MB
    def rows_step(m, _):
        rows = pl.ds(pl.multiple_of(m * mb, mb), mb)
        xm = x[rows]
        v = jnp.dot(xm, wgu[0], preferred_element_type=f32).astype(bf16).astype(f32)
        u = jnp.dot(xm, wgu[1], preferred_element_type=f32).astype(bf16).astype(f32)
        dh = lax.dot_general(g[rows], wd[...], NT, preferred_element_type=f32)
        sq = v * v
        half = 0.5 + 0.5 * jnp.tanh(v * (ROOT + (ROOT * 0.044715) * sq))
        act = v * half
        slope = half + (2.0 * v * half) * ((1.0 - half) * (ROOT + (3 * 0.044715 * ROOT) * sq))
        h = (act * u).astype(bf16)
        hid[rows] = h
        dga[rows] = (dh * u * slope).astype(bf16)
        dup[rows] = (dh * act).astype(bf16)
        hidt[:, rows] = h.T
        return 0
    lax.fori_loop(0, tokens // mb, rows_step, 0)
    c_out = [copies.start(hid, hid_h), copies.start(dga, dg_h), copies.start(dup, du_h)]
    block = own_down.shape[1]
    half_block = block // 2
    def down_step(b, _):
        rows = pl.ds(pl.multiple_of(b * block, 16), block)
        gd[rows] = jnp.dot(hidt[rows], g[...], preferred_element_type=f32).astype(bf16)
        return 0
    lax.fori_loop(0, groups, down_step, 0)
    for b in range(groups):
        for side, dst in ((core, gdm_h), (1 - core, gdo_h)):
            c_out.append(copies.start(gd.at[pl.ds(pl.multiple_of(b * block + side * half_block, 8), half_block)], dst.at[b]))
    c_xt.wait()
    block = own_gate.shape[1]
    for i, act in ((0, dga), (1, dup)):
        def gate_step(b, _, i=i, act=act):
            rows = pl.ds(pl.multiple_of(b * block, 16), block)
            ggu[i, rows] = jnp.dot(xt[rows], act[...], preferred_element_type=f32).astype(bf16)
            return 0
        lax.fori_loop(0, groups, gate_step, 0)
    c_out.append(copies.start(ggu.at[core], gm_h))
    c_out.append(copies.start(ggu.at[1 - core], go_h))
    wait(c_out)

def ffn_chunk(scal, x, xt, g, own_gate, own_up, own_down, gate_up, down):
    tokens, d = x.shape
    groups = d // own_gate.shape[1]
    f = own_gate.shape[2]
    n_gu, arrays_gu, copies_gu = parts_of(gate_up)
    n_d, arrays_d, copies_d = parts_of(down)
    nparts = (n_gu, n_d)
    act = jax.ShapeDtypeStruct((tokens, f), bf16)
    gu = jax.ShapeDtypeStruct((d, f), bf16)
    gdn = jax.ShapeDtypeStruct((groups, own_down.shape[1] // 2, d), bf16)
    ins = [x, xt, g, own_gate, own_up, own_down, *arrays_gu, *arrays_d]
    ncop = 3 + copies_gu + copies_d + 3 + 2 * groups + 2
    V = lambda s: pltpu.VMEM(s, bf16)
    return pl.pallas_call(
        functools.partial(ffn_kernel, groups, nparts),
        in_specs=[pl.BlockSpec(memory_space=pltpu.SMEM)] + [ANY] * len(ins),
        out_specs=[ANY] * 7,
        out_shape=[act, act, act, gu, gu, gdn, gdn],
        scratch_shapes=[V((tokens, d)), V((d, tokens)), V((tokens, d)), V((2, d, f)), V((f, d)), V((tokens, f)), V((tokens, f)), V((tokens, f)), V((f, tokens)), V((2, d, f)), V((f, d)), pltpu.SemaphoreType.DMA((ncop,))],
        compiler_params=pltpu.CompilerParams(vmem_limit_bytes=VMEM_LIMIT),
        cost_estimate=kernel_cost(30),
        name="ffn_chunk",
    )(scal, *ins)

TB = 256


def norm_back_columns(values, gain, grad):
    r = lax.rsqrt(jnp.mean(values * values, axis=0, keepdims=True) + FLOOR)
    scaled = gain * grad
    back = r * scaled - values * ((r * r * r) * jnp.mean(scaled * values, axis=0, keepdims=True))
    return back, jnp.sum(grad * values * r, axis=1, keepdims=True)


def dx_kernel(groups, counts, *refs):
    it = iter(refs)
    scal = next(it)
    gain_h, middle_h, g_h = next(it), next(it), next(it)
    own_gate, own_up = next(it), next(it)
    chunks = []
    for n in counts:
        dg, du = next(it), next(it)
        chunks.append((dg, du, *take_parts(it, n)))
    dm_h, da_h, gg_h = next(it), next(it), next(it)
    acc, wgu, dga, dup, middle, g, gain, gg, sems = [next(it) for _ in range(9)]
    copies = Copies(sems)
    tokens = acc.shape[1]

    def load(j):
        dg, du, mine, other = chunks[j]
        s = (scal[0], scal[1] ^ j, scal[2])
        out = load_gate_up(copies, s, wgu.at[j % 2], own_gate, own_up, mine, other, groups)
        return out + [copies.start(dg, dga.at[j % 2]), copies.start(du, dup.at[j % 2])]

    pending = load(0)
    extra = [copies.start(gain_h, gain), copies.start(middle_h, middle), copies.start(g_h, g)]
    for j in range(len(chunks)):
        following = load(j + 1) if j + 1 < len(chunks) else []
        wait(pending)
        pending = following
        b = j % 2

        def step(m, _, j=j, b=b):
            at = pl.ds(pl.multiple_of(m * MB, MB), MB)
            part = lax.dot_general(wgu[b, 0], dga[b, at], NT, preferred_element_type=f32)
            part += lax.dot_general(wgu[b, 1], dup[b, at], NT, preferred_element_type=f32)
            acc[:, at] = part if j == 0 else acc[:, at] + part
            return 0

        lax.fori_loop(0, tokens // MB, step, 0)
    wait(extra)
    gg[...] = jnp.zeros_like(gg)

    def finish(m, _):
        at = pl.ds(pl.multiple_of(m * TB, TB), TB)
        back, part = norm_back_columns(middle[:, at], gain[...], acc[:, at])
        total = g[:, at].astype(f32) + back
        acc[:, at] = total
        g[:, at] = total.astype(bf16)
        gg[...] += part
        return 0

    lax.fori_loop(0, tokens // TB, finish, 0)
    wait([copies.start(g, da_h), copies.start(acc, dm_h), copies.start(gg, gg_h)])


def ffn_dx(scal, gain, middle_t, g_t, own_gate, own_up, chunks):
    tokens, f = chunks[0][0].shape
    d = middle_t.shape[0]
    groups = d // own_gate.shape[1]
    ins = [gain, middle_t, g_t, own_gate, own_up]
    ncop = 6
    counts = []
    for dg, du, source in chunks:
        n, arrays, copies = parts_of(source)
        counts.append(n)
        ins += [dg, du, *arrays]
        ncop += 2 + copies
    V = lambda s: pltpu.VMEM(s, bf16)
    F = lambda s: pltpu.VMEM(s, f32)
    return pl.pallas_call(
        functools.partial(dx_kernel, groups, tuple(counts)),
        in_specs=[pl.BlockSpec(memory_space=pltpu.SMEM)] + [ANY] * len(ins),
        out_specs=[ANY, ANY, ANY],
        out_shape=[jax.ShapeDtypeStruct((d, tokens), f32), jax.ShapeDtypeStruct((d, tokens), bf16), jax.ShapeDtypeStruct((d, 1), f32)],
        scratch_shapes=[F((d, tokens)), V((2, 2, d, f)), V((2, tokens, f)), V((2, tokens, f)), F((d, tokens)), V((d, tokens)), F((d, 1)), F((d, 1)), pltpu.SemaphoreType.DMA((ncop,))],
        compiler_params=pltpu.CompilerParams(vmem_limit_bytes=VMEM_LIMIT),
        cost_estimate=kernel_cost(35),
        name="ffn_dx",
    )(scal, *ins)


def middle_kernel(ctx_ref, w_ref, x_ref, gain_ref, mid_ref, nt_ref, n_ref):
    mid = x_ref[...].astype(f32) + lax.dot_general(w_ref[...], ctx_ref[...], NT, preferred_element_type=f32)
    mid_ref[...] = mid
    normed = mid * lax.rsqrt(jnp.mean(mid * mid, axis=0, keepdims=True) + FLOOR) * gain_ref[...]
    nt_ref[...] = normed.astype(bf16)
    n_ref[...] = normed.T.astype(bf16)


def middle_norm(context, wo_t, x_t, gain):
    d, tokens = x_t.shape
    width = context.shape[1]
    cols = pl.BlockSpec((d, TB), lambda i: (0, i))
    return pl.pallas_call(
        middle_kernel,
        grid=(tokens // TB,),
        in_specs=[pl.BlockSpec((TB, width), lambda i: (i, 0)), pl.BlockSpec((d, width), lambda i: (0, 0)), cols, pl.BlockSpec((d, 1), lambda i: (0, 0))],
        out_specs=[cols, cols, pl.BlockSpec((TB, d), lambda i: (i, 0))],
        out_shape=[jax.ShapeDtypeStruct((d, tokens), f32), jax.ShapeDtypeStruct((d, tokens), bf16), jax.ShapeDtypeStruct((tokens, d), bf16)],
        compiler_params=pltpu.CompilerParams(vmem_limit_bytes=VMEM_LIMIT),
        cost_estimate=kernel_cost(7),
        name="middle_norm",
    )(context, wo_t, x_t, gain)


def input_kernel(dq_ref, dk_ref, dv_ref, w_ref, x_ref, dm_ref, gain_ref, out_ref, gg_ref):
    grads = jnp.concatenate([dq_ref[...], dk_ref[...], dv_ref[...]], axis=1)
    d_normed = lax.dot_general(w_ref[...], grads, NT, preferred_element_type=f32)
    back, part = norm_back_columns(x_ref[...].astype(f32), gain_ref[...], d_normed)
    out_ref[...] = (dm_ref[...] + back).astype(bf16)

    @pl.when(pl.program_id(0) == 0)
    def _():
        gg_ref[...] = jnp.zeros_like(gg_ref)

    gg_ref[...] += part


def input_gradient(dq, dk, dv, wqkv, x_t, dm_t, gain):
    d, tokens = x_t.shape
    width = dq.shape[1]
    head = pl.BlockSpec((TB, width), lambda i: (i, 0))
    cols = pl.BlockSpec((d, TB), lambda i: (0, i))
    one = pl.BlockSpec((d, 1), lambda i: (0, 0))
    return pl.pallas_call(
        input_kernel,
        grid=(tokens // TB,),
        in_specs=[head, head, head, pl.BlockSpec((d, 3 * width), lambda i: (0, 0)), cols, cols, one],
        out_specs=[cols, one],
        out_shape=[jax.ShapeDtypeStruct((d, tokens), bf16), jax.ShapeDtypeStruct((d, 1), f32)],
        compiler_params=pltpu.CompilerParams(vmem_limit_bytes=VMEM_LIMIT),
        cost_estimate=kernel_cost(8),
        name="input_gradient",
    )(dq, dk, dv, wqkv, x_t, dm_t, gain)


def matrices_kernel(groups, *refs):
    scal, nt_h, dq_h, dk_h, dv_h, ctx_h, da_h, small_h, mine_h, other_h = refs[:10]
    nt, dqkv, ctx, ctx_t, da, small, buf, sems = refs[10:]
    d, tokens = nt.shape
    width = ctx.shape[1]
    rows = d // groups
    half = width // 2
    copies = Copies(sems)
    c_out = [copies.start(ctx_h, ctx), copies.start(da_h, da)]
    c_in = [copies.start(nt_h, nt), copies.start(small_h, small)]
    c_in += [copies.start(src, dqkv.at[m]) for m, src in enumerate((dq_h, dk_h, dv_h))]
    wait(c_out)
    ctx_t[...] = ctx[...].T
    grad_out = lax.dot_general(ctx_t[...], da[...], NT, preferred_element_type=f32).astype(bf16)
    n = width // groups
    for z in range(groups):
        for i in range(4):
            block = grad_out[z * n : (z + 1) * n, i * width : min(d, (i + 1) * width)]
            if block.shape[1] < width:
                block = jnp.concatenate([block, jnp.zeros((n, width - block.shape[1]), bf16)], axis=1)
            buf[i // 2, 3, z, (i % 2) * n : (i % 2 + 1) * n] = block
    wait(c_in)
    for m in range(3):

        def step(z, _, m=m):
            part = jnp.dot(nt[pl.ds(pl.multiple_of(z * rows, 16), rows)], dqkv[m], preferred_element_type=f32).astype(bf16)
            buf[0, m, z] = part[:half]
            buf[1, m, z, : rows - half] = part[half:]
            buf[1, m, z, rows - half :] = small[z]
            return 0

        lax.fori_loop(0, groups, step, 0)
    wait([copies.start(buf.at[scal[2]], mine_h), copies.start(buf.at[1 - scal[2]], other_h)])


def attention_matrices(scal, normed_t, dq, dk, dv, ctx, da_t, small):
    d, tokens = normed_t.shape
    groups = small.shape[0]
    width = dq.shape[1]
    out = jax.ShapeDtypeStruct((4, groups, width // 2, width), bf16)
    V = lambda s: pltpu.VMEM(s, bf16)
    return pl.pallas_call(
        functools.partial(matrices_kernel, groups),
        in_specs=[pl.BlockSpec(memory_space=pltpu.SMEM)] + [ANY] * 7,
        out_specs=[ANY, ANY],
        out_shape=[out, out],
        scratch_shapes=[V((d, tokens)), V((3, tokens, width)), V((tokens, width)), V((width, tokens)), V((d, tokens)), V(small.shape), V((2, *out.shape)), pltpu.SemaphoreType.DMA((9,))],
        compiler_params=pltpu.CompilerParams(vmem_limit_bytes=VMEM_LIMIT),
        cost_estimate=kernel_cost(9),
        name="attention_matrices",
    )(scal, normed_t, dq, dk, dv, ctx, da_t, small)


def out_kernel(groups, counts, *refs):
    it = iter(refs)
    scal = next(it)
    middle, own_down = next(it), next(it)
    chunks = []
    for n in counts:
        hid = next(it)
        chunks.append((hid, *take_parts(it, n)))
    out_h = next(it)
    acc, mid, out, wd, act, sems = [next(it) for _ in range(6)]
    copies = Copies(sems)

    def load(j):
        hid, mine, other = chunks[j]
        s = (scal[0], scal[1] ^ j, scal[2])
        return load_down(copies, s, wd.at[j % 2], own_down, mine, other, groups) + [copies.start(hid, act.at[j % 2])]

    c_middle = copies.start(middle, mid)
    pending = load(0)
    for j in range(len(chunks)):
        following = load(j + 1) if j + 1 < len(chunks) else []
        wait(pending)
        pending = following
        b = j % 2

        def step(m, _, j=j, b=b):
            rows = pl.ds(pl.multiple_of(m * MB, MB), MB)
            part = jnp.dot(act[b, rows], wd[b], preferred_element_type=f32)
            acc[rows] = part if j == 0 else acc[rows] + part
            return 0

        lax.fori_loop(0, acc.shape[0] // MB, step, 0)
    c_middle.wait()

    def finish(m, _):
        at = pl.ds(pl.multiple_of(m * TB, TB), TB)
        out[:, at] = (mid[:, at] + acc[at].T).astype(bf16)
        return 0

    lax.fori_loop(0, acc.shape[0] // TB, finish, 0)
    done = copies.start(out, out_h)
    done.wait()


def ffn_out(scal, middle, own_down, chunks):
    d, tokens = middle.shape
    f = chunks[0][0].shape[1]
    groups = f // own_down.shape[1]
    ins = [middle, own_down]
    ncop = 2
    counts = []
    for hid, source in chunks:
        n, arrays, copies = parts_of(source)
        counts.append(n)
        ins += [hid, *arrays]
        ncop += 1 + copies
    V = lambda s: pltpu.VMEM(s, bf16)
    return pl.pallas_call(
        functools.partial(out_kernel, groups, tuple(counts)),
        in_specs=[pl.BlockSpec(memory_space=pltpu.SMEM)] + [ANY] * len(ins),
        out_specs=ANY,
        out_shape=jax.ShapeDtypeStruct((d, tokens), bf16),
        scratch_shapes=[pltpu.VMEM((tokens, d), f32), pltpu.VMEM((d, tokens), f32), V((d, tokens)), V((2, f, d)), V((2, tokens, f)), pltpu.SemaphoreType.DMA((ncop,))],
        compiler_params=pltpu.CompilerParams(vmem_limit_bytes=VMEM_LIMIT),
        cost_estimate=kernel_cost(21),
        name="ffn_out",
    )(scal, *ins)


def split_kernel(gate_ref, up_ref, og_ref, ou_ref):
    quarter = og_ref.shape[0]
    width = og_ref.shape[2] // quarter
    for src, dst in ((gate_ref, og_ref), (up_ref, ou_ref)):
        for p in range(quarter):
            for b in range(quarter):
                at = (b * quarter + p) * width
                dst[p, :, b * width : (b + 1) * width] = src[:, at : at + width]


def split_columns(gate, up):
    rows, ff = gate.shape
    tile = rows // 2
    out = jax.ShapeDtypeStruct((4, rows, ff // 4), bf16)
    return pl.pallas_call(
        split_kernel,
        grid=(2,),
        in_specs=[pl.BlockSpec((tile, ff), lambda i: (i, 0))] * 2,
        out_specs=[pl.BlockSpec((4, tile, ff // 4), lambda i: (0, i, 0))] * 2,
        out_shape=[out, out],
        cost_estimate=kernel_cost(5),
        name="split_columns",
    )(gate, up)


def join_kernel(scal, *refs):
    mine, other, gate_ref, up_ref = refs
    me, core = scal[1], scal[2]
    width = mine.shape[2] // 4

    def put(p, j, side):
        for src, dst in ((mine, (gate_ref, up_ref)[side]), (other, (gate_ref, up_ref)[1 - side])):
            for b in range(4):
                at = (b * 4 + p) * width
                dst[:, at : at + width] = src[j, :, b * width : (b + 1) * width].astype(f32)

    for own in range(4):
        for side in range(2):

            @pl.when(jnp.logical_and(me == own, core == side))
            def _(own=own, side=side):
                for j in range(4):
                    put(own ^ j, j, side)


def join_columns(scal, mine, other):
    _, rows, f = mine.shape
    tile = rows // 2
    out = jax.ShapeDtypeStruct((rows, 4 * f), f32)
    return pl.pallas_call(
        join_kernel,
        grid=(2,),
        in_specs=[pl.BlockSpec(memory_space=pltpu.SMEM)] + [pl.BlockSpec((4, tile, f), lambda i: (0, i, 0))] * 2,
        out_specs=[pl.BlockSpec((tile, 4 * f), lambda i: (i, 0))] * 2,
        out_shape=[out, out],
        cost_estimate=kernel_cost(6.5),
        compiler_params=pltpu.CompilerParams(vmem_limit_bytes=VMEM_LIMIT),
        name="join_columns",
    )(scal, mine, other)


def weights_kernel(groups, *refs):
    scal = refs[0]
    mine, other = refs[1:5], refs[5:9]
    wqkv, wo, smalls, buf, flat, sems = refs[9:]
    rows = wqkv.shape[0] // groups
    width = buf.shape[-1]
    half = width // 2
    out_rows = width // groups
    d = wo.shape[0]
    copies = Copies(sems)
    done = []
    for j in range(4):
        for side, arrays in ((scal[2], mine), (1 - scal[2], other)):
            for k in range(groups):
                z = lax.rem(scal[0] - k + groups, groups)
                done.append(copies.start(arrays[j].at[k], buf.at[scal[1] ^ j, z, pl.ds(pl.multiple_of(side * half, 16), half)]))
    wait(done)
    for z in range(groups):
        for m in range(3):
            wqkv[z * rows : (z + 1) * rows, m * width : (m + 1) * width] = buf[m, z, :rows]
        for i in range(-(-d // width)):
            n = min(width, d - i * width)
            flat[z * out_rows : (z + 1) * out_rows, i * width : i * width + n] = buf[3, z, i * out_rows : (i + 1) * out_rows, :n]
        smalls[z] = buf[0, z, rows:]
    wo[...] = flat[...].T


def attention_weights(scal, mine, other, rows, d):
    groups, half, width = mine[0].shape
    V = pl.BlockSpec(memory_space=pltpu.VMEM)
    return pl.pallas_call(
        functools.partial(weights_kernel, groups),
        in_specs=[pl.BlockSpec(memory_space=pltpu.SMEM)] + [ANY] * 8,
        out_specs=[V, V, V],
        out_shape=[
            jax.ShapeDtypeStruct((groups * rows, 3 * width), bf16),
            jax.ShapeDtypeStruct((d, width), bf16),
            jax.ShapeDtypeStruct((groups, width - rows, width), bf16),
        ],
        scratch_shapes=[pltpu.VMEM((4, groups, width, width), bf16), pltpu.VMEM((width, d), bf16), pltpu.SemaphoreType.DMA((8 * groups,))],
        cost_estimate=kernel_cost(5.8),
        compiler_params=pltpu.CompilerParams(vmem_limit_bytes=VMEM_LIMIT),
        name="attention_weights",
    )(scal, *mine, *other)


def gradients_kernel(*refs):
    scal = refs[0]
    mine, other = refs[1:3]
    grads, grad_out, small, buf, sems = refs[3], refs[4], refs[5], refs[6], refs[7]
    rows = grads.shape[1]
    width = buf.shape[-1]
    half = width // 2
    out_rows, d = grad_out.shape
    copies = Copies(sems)
    done = []
    for j in range(4):
        for side, arrays in ((scal[2], mine), (1 - scal[2], other)):
            done.append(copies.start(arrays.at[j], buf.at[scal[1] ^ j, pl.ds(pl.multiple_of(side * half, 16), half)]))
    wait(done)
    for m in range(3):
        grads[m] = buf[m, :rows].astype(f32)
    for i in range(-(-d // width)):
        n = min(width, d - i * width)
        grad_out[:, i * width : i * width + n] = buf[3, i * out_rows : (i + 1) * out_rows, :n].astype(f32)
    small[...] = buf[0, rows:].astype(f32)


def attention_gradients(scal, mine, other, rows, out_rows, d):
    _, half, width = mine.shape
    V = pl.BlockSpec(memory_space=pltpu.VMEM)
    return pl.pallas_call(
        gradients_kernel,
        in_specs=[pl.BlockSpec(memory_space=pltpu.SMEM)] + [ANY] * 2,
        out_specs=[V, V, V],
        out_shape=[
            jax.ShapeDtypeStruct((3, rows, width), f32),
            jax.ShapeDtypeStruct((out_rows, d), f32),
            jax.ShapeDtypeStruct((width - rows, width), f32),
        ],
        scratch_shapes=[pltpu.VMEM((4, width, width), bf16), pltpu.SemaphoreType.DMA((8,))],
        cost_estimate=kernel_cost(3.5),
        compiler_params=pltpu.CompilerParams(vmem_limit_bytes=VMEM_LIMIT),
        name="attention_gradients",
    )(scal, mine, other)


def down_kernel(*refs):
    scal = refs[0]
    mine, other = refs[1:3]
    out, buf, sems = refs[3:]
    half = buf.shape[0] // 8
    copies = Copies(sems)
    done = []
    for j in range(4):
        for side, arrays in ((scal[2], mine), (1 - scal[2], other)):
            at = ((scal[1] ^ j) * 2 + side) * half
            done.append(copies.start(arrays.at[j], buf.at[pl.ds(pl.multiple_of(at, 16), half)]))
    wait(done)
    for i in range(buf.shape[0] // 128):
        rows = slice(i * 128, (i + 1) * 128)
        out[:, rows] = buf[rows].astype(f32).T


def down_gradient(scal, mine, other):
    _, half, d = mine.shape
    return pl.pallas_call(
        down_kernel,
        in_specs=[pl.BlockSpec(memory_space=pltpu.SMEM)] + [ANY] * 2,
        out_specs=pl.BlockSpec(memory_space=pltpu.VMEM),
        out_shape=jax.ShapeDtypeStruct((d, 8 * half), f32),
        scratch_shapes=[pltpu.VMEM((8 * half, d), bf16), pltpu.SemaphoreType.DMA((8,))],
        cost_estimate=kernel_cost(5.6),
        compiler_params=pltpu.CompilerParams(vmem_limit_bytes=VMEM_LIMIT),
        name="down_gradient",
    )(scal, mine, other)


def dot(left, right, form):
    return jnp.einsum(form, left, right, preferred_element_type=f32)


def add(*terms):
    total = terms[0].astype(f32)
    for term in terms[1:]:
        total = total + term.astype(f32)
    return total.astype(bf16)


def after(v, *others):
    return lax.optimization_barrier((v, others))[0]


def pick(stack, i):
    return lax.dynamic_index_in_dim(stack, i, 0, keepdims=False)


SHARD = ("outer", "chip", "core")


class Links:
    def __init__(self, shards, groups):
        self.shards, self.groups = shards, groups
        self.z = lax.axis_index("group")
        self.index = lax.axis_index(SHARD)
        self.core = self.index & 1
        self.chip = (self.index >> 1) & 3

    def swap(self, v, bit):
        return lax.ppermute(v, SHARD, [(i, i ^ bit) for i in range(self.shards)])

    def turn(self, v, k):
        return lax.ppermute(v, "group", [(i, (i + k) % self.groups) for i in range(self.groups)])

    def ring_gather(self, v):
        return [v] + [self.turn(v, k) for k in range(1, self.groups)]

    def others(self, v):
        return jnp.stack([pick(v, (self.z - k) % self.groups) for k in range(1, self.groups)])

    def ring_reduce(self, v, *others):
        at = lambda k: pick(v, (self.z + k) % self.groups)
        total = at(0).astype(f32)
        for k in range(1, self.groups):
            total = total + after(self.turn(at(k), k), *others).astype(f32)
        return total

    def beyond(self, total):
        bit = 8
        while bit < self.shards:
            total = total + self.swap(total, bit)
            bit *= 2
        return total


def local(
    layer_input_rows,
    gain_attn,
    w_query,
    w_key,
    w_value,
    w_out,
    gain_ff,
    gate_weight,
    w_up,
    w_down,
    bucket_head_bias,
    positions,
    rel_bucket,
    out_grad,
    *,
    shards,
    groups,
):
    links = Links(shards, groups)
    z, core, chip = links.z, links.core, links.chip
    tokens, d = layer_input_rows.shape
    seqs = tokens // SEQ
    width = w_query.shape[1]
    rows = w_query.shape[0]
    buckets = bucket_head_bias.shape[0] * groups
    scals = [jnp.stack([z, chip ^ j, core]).astype(jnp.int32) for j in range(4)]
    scal = scals[0]

    small = jnp.concatenate([gain_attn, gain_ff, bucket_head_bias.reshape(-1)])
    spare = width - rows
    small = jnp.pad(small, (0, spare * width - small.shape[0])).reshape(spare, width)
    out_blocks = -(-d // width)
    wo_block = jnp.pad(w_out, ((0, 0), (0, out_blocks * width - d)))
    wo_block = jnp.concatenate([wo_block[:, i * width : (i + 1) * width] for i in range(out_blocks)])
    tall = lambda w: jnp.concatenate([w, small])
    four = jnp.stack([tall(w_query), tall(w_key), tall(w_value), wo_block])
    half = width // 2
    piece = lax.dynamic_slice(four, (chip, core * half, 0), (1, half, width))[0]
    slots = links.ring_gather(piece)
    own_gate, own_up = split_columns(gate_weight, w_up)
    slots[1:] = after(slots[1:], own_gate)
    mine = [jnp.stack(slots)]
    x_t, g_t = layer_input_rows.T, out_grad.T
    g = lax.optimization_barrier(out_grad)
    arrived = [links.swap(mine[0], bit) for bit in (XBIT, YBIT, XBIT | YBIT)]
    mine += [after(a, g) for a in arrived]
    wqkv, wo_t, smalls = attention_weights(scal, mine, [links.swap(a, CORE) for a in mine], rows, d)
    smalls = smalls.reshape(groups, -1)
    gains = [smalls[:, i * rows : (i + 1) * rows].reshape(d, 1).astype(f32) for i in range(2)]
    bias_table = smalls[:, 2 * rows : 2 * rows + bucket_head_bias.size].reshape(buckets, H)

    own_down = w_down.reshape(4, -1, d)
    half_down = own_down.shape[1] // 2
    whole = lambda v: lax.all_gather(v, ("core", "group")).reshape(2, groups, *v.shape)
    gate_up_of = lambda p: jnp.where(core == 0, pick(own_gate, p), pick(own_up, p))
    down_of = lambda p: lax.dynamic_slice(own_down, (p, core * half_down, 0), (1, half_down, d))[0]
    near_gu = whole(after(gate_up_of(chip), *slots[1:]))

    inputs = x_t.astype(f32)
    r_attn = lax.rsqrt(jnp.mean(inputs * inputs, axis=0, keepdims=True) + FLOOR)
    normed_t = (inputs * r_attn * gains[0]).astype(bf16)
    qkv = dot(normed_t, wqkv, "dt,dc->tc").astype(bf16)
    onehot = (rel_bucket[:, None] == jnp.arange(buckets, dtype=jnp.int32)[None, :]).astype(f32)
    offsets = jnp.dot(onehot, bias_table.astype(f32), precision=lax.Precision.HIGHEST).T
    bias = bias_matrix(offsets[:, None, :])
    near_dn = whole(after(down_of(chip), bias))
    places = (positions // BLOCK).reshape(seqs, SEQ)
    attend, context = attend_forward(qkv, after(bias, near_gu), places[:, :, None], places[:, None, :])
    gu = links.others(pick(after(near_gu, context), core))
    gu_x, gu_y = links.swap(gu, XBIT), links.swap(gu, YBIT)
    middle_t, normed_ff_t, normed_ff = middle_norm(context, wo_t, x_t, gains[1])
    dn = links.others(pick(after(near_dn, context), core))
    dn_x, dn_y = links.swap(dn, XBIT), links.swap(dn, YBIT)
    far_gu, far_dn = whole(after(gate_up_of(chip ^ 3), qkv)), whole(after(down_of(chip ^ 3), context))
    gus, dns = [near_gu], [near_dn]
    both = lambda parts: (parts, [links.swap(a, CORE) for a in parts])

    acts, sums_gu, sums_dn = [None] * 4, [None] * 4, [None] * 4

    def chunk(j, *deps):
        hid, dg, du, gm, go, dm, do = ffn_chunk(
            after(scals[j], *deps), normed_ff, normed_ff_t, g, own_gate, own_up, own_down, gus[j], dns[j]
        )
        acts[j] = (hid, dg, du)
        sums_gu[j] = add(gm, links.swap(go, CORE))
        sums_dn[j] = add(dm, links.swap(do, CORE))
        return hid

    n = d // 2
    scatter = lambda v: lax.psum_scatter(v, "group", scatter_dimension=0)
    done = chunk(0)
    gu_x, gu_y, dn_x, dn_y = after((gu_x, gu_y, dn_x, dn_y), done)
    gus += [both([gu_x]), both([gu_y])]
    dns += [both([dn_x]), both([dn_y])]
    gus.append(far_gu)
    dns.append(far_dn)
    rings = [None] * 4
    rings[0] = scatter(sums_dn[0])
    done = chunk(1, done, sums_dn[0], far_gu)
    rings[1] = scatter(sums_dn[1])
    done = chunk(2, done, sums_gu[0], sums_dn[1], rings[0], far_dn)
    rings[2] = scatter(sums_dn[2])
    done = chunk(3, done, sums_gu[1], sums_dn[2], rings[1])
    from_x = [links.swap(sums_gu[1][:n], XBIT), links.swap(sums_gu[1][n:], XBIT)]
    from_y = [links.swap(sums_gu[2][:n], YBIT), links.swap(sums_gu[2][n:], YBIT)]
    rings[3] = scatter(sums_dn[3])
    far_sum = scatter(sums_gu[3].reshape(groups, rows, -1))
    d_middle_t, d_attn_t, grad_gain_ff = ffn_dx(
        after(scal, done, rings[2], sums_gu[2], sums_gu[3], sums_dn[2], sums_dn[3]),
        gains[1],
        middle_t,
        g_t,
        own_gate,
        own_up,
        [(acts[j][1], acts[j][2], gus[j]) for j in range(4)],
    )
    d_attn_t = after(d_attn_t, from_x[0], from_y[0], rings[3])
    d_context = dot(d_attn_t, wo_t, "dt,dc->tc").astype(bf16)
    d_q, d_k, d_v, per_offset = attend_backward(qkv, attend, d_context)
    far = after([links.swap(rings[j], j << 1) for j in (1, 2, 3)], d_q)
    from_x[1], from_y[1] = after((from_x[1], from_y[1]), d_q)
    red_dn = rings[0].astype(f32)
    for part in far:
        red_dn = red_dn + part.astype(f32)
    red_dn = links.beyond(red_dn).astype(bf16)
    red_gu = jnp.concatenate([add(sums_gu[0][:n], from_x[0], from_y[0]), add(sums_gu[0][n:], from_x[1], from_y[1])])
    d_q = after(d_q, red_dn, red_gu)
    red_gu = scatter(red_gu.reshape(groups, rows, -1))
    grad_table = jnp.dot(onehot.T, per_offset[:, 0, :].T, precision=lax.Precision.HIGHEST)
    input_grad_t, grad_gain_attn = input_gradient(d_q, d_k, d_v, wqkv, x_t, d_middle_t, gains[0])

    small = [grad_gain_attn.reshape(groups, -1), grad_gain_ff.reshape(groups, -1), grad_table.reshape(groups, -1)]
    small = jnp.concatenate(small, axis=1).astype(bf16)
    small = jnp.pad(small, ((0, 0), (0, spare * width - small.shape[1]))).reshape(groups, spare, width)
    mine, other = attention_matrices(after(scal, input_grad_t), normed_t, d_q, d_k, d_v, context, d_attn_t, small)
    sums = add(mine, links.swap(other, CORE))

    def spread(v, *others):
        received = [after(links.swap(v, j << 1), *others) for j in (1, 2, 3)]
        mine = jnp.stack([v, *received])
        return mine, links.swap(mine, CORE)

    spread_dn = spread(red_dn, mine)
    far_sum = links.swap(far_sum, XBIT | YBIT)
    red_gu = links.beyond(red_gu.astype(f32) + after(far_sum, mine).astype(f32)).astype(bf16)
    gu_x, gu_y = links.swap(red_gu, XBIT), links.swap(red_gu, YBIT)
    output_t = ffn_out(after(scal, sums, spread_dn[1], red_gu), middle_t, own_down, [(acts[j][0], dns[j]) for j in range(4)])
    gu_x, gu_y = after((gu_x, gu_y), output_t)
    red_plane = add(pick(sums, chip), *(after(links.swap(pick(sums, chip ^ j), j << 1), output_t) for j in (1, 2, 3)))
    red = links.beyond(scatter(red_plane).astype(f32)).astype(bf16)
    mid = rows // 2
    gu_d = jnp.concatenate([links.swap(gu_x[:mid], YBIT), links.swap(gu_y[mid:], XBIT)])
    spread_gu = jnp.stack([red_gu, gu_x, gu_y, gu_d])
    grad_gate, grad_up = join_columns(scal, spread_gu, links.swap(spread_gu, CORE))
    grad_down = down_gradient(scal, *after(spread_dn, red_plane)).T
    wide, grad_out, small = attention_gradients(scal, *spread(red), rows, *w_out.shape)
    small = small.reshape(-1)
    return (
        output_t.T,
        input_grad_t.T,
        small[:rows],
        wide[0],
        wide[1],
        wide[2],
        grad_out,
        small[rows : 2 * rows],
        grad_gate,
        grad_up,
        grad_down,
        small[2 * rows : 2 * rows + bucket_head_bias.size].reshape(bucket_head_bias.shape),
    )


def solution(mesh):
    shards, groups = mesh.shape["shard"], mesh.shape["group"]
    mesh = jax.sharding.Mesh(mesh.devices.reshape(shards // 8, 4, 2, groups), (*SHARD, "group"))
    split = P((*SHARD, "group"), None)
    rows = P("group", None)
    in_specs = (split, P("group"), rows, rows, rows, rows, P("group"), rows, rows, rows, rows, P((*SHARD, "group")), P(), split)
    out_specs = (split, split, P("group"), rows, rows, rows, rows, P("group"), rows, rows, rows, rows)
    body = functools.partial(local, shards=shards, groups=groups)
    return jax.shard_map(body, mesh=mesh, in_specs=in_specs, out_specs=out_specs, check_vma=False)
```

```python
import functools

import jax
import jax.numpy as jnp
from jax import lax
from jax.experimental import pallas as pl
from jax.experimental.pallas import tpu as pltpu
from jax.sharding import PartitionSpec as P

H = 6
DK = 64
SEQ = 512
BLOCK = 256
FLOOR = 1e-06
ROOT = 0.7978845608028654
CUBIC = 0.044715
RB = 128
MB = 512
VMEM_LIMIT = 60 << 20
NT = (((1,), (1,)), ((), ()))
TN = (((0,), (0,)), ((), ()))
ANY = pl.BlockSpec(memory_space=pl.ANY)
bf16 = jnp.bfloat16
f32 = jnp.float32
CORE, XBIT, YBIT = 1, 2, 4


def kernel_cost(us):
    return pl.CostEstimate(flops=int(us * 1.15e9), bytes_accessed=int(us * 1e6), transcendentals=0)


def skew_bias(off_ref, bias_ref):
    rows = jnp.broadcast_to(off_ref[0], (SEQ, 2 * SEQ))
    bias_ref[0] = pltpu.roll(rows, SEQ, 1, stride=1, stride_axis=0)[:, :SEQ].astype(bias_ref.dtype)


def bias_matrix(offsets):
    return pl.pallas_call(
        skew_bias,
        grid=(H,),
        in_specs=[pl.BlockSpec((1, 1, 2 * SEQ), lambda h: (h, 0, 0))],
        out_specs=pl.BlockSpec((1, SEQ, SEQ), lambda h: (h, 0, 0)),
        out_shape=jax.ShapeDtypeStruct((H, SEQ, SEQ), bf16),
        cost_estimate=kernel_cost(4),
        name="bias_matrix",
    )(offsets)


def half_lanes(v, side):
    lane = lax.broadcasted_iota(jnp.int32, v.shape, 1)
    return jnp.where((lane < DK) == (side == 0), v, jnp.zeros_like(v))


def attend_kernel(q_ref, k_ref, v_ref, bias_ref, row_ref, col_ref, attend_ref, ctx_ref):
    keys = k_ref[...]
    values = v_ref[...]
    col = col_ref[0]
    for b in range(SEQ // RB):
        rows = pl.ds(b * RB, RB)
        allowed = col <= row_ref[0, rows]
        ctx = None
        for side in range(2):
            s = lax.dot_general(half_lanes(q_ref[rows], side), keys, NT, preferred_element_type=f32)
            s = jnp.where(allowed, s + bias_ref[side, rows].astype(f32), -1e30)
            p = jnp.exp(s - jnp.max(s, axis=-1, keepdims=True))
            p = (p * (1.0 / jnp.sum(p, axis=-1, keepdims=True))).astype(bf16)
            attend_ref[0, side, rows] = p
            part = half_lanes(jnp.dot(p, values, preferred_element_type=f32), side)
            ctx = part if ctx is None else ctx + part
        ctx_ref[rows] = ctx.astype(bf16)


def pair(which):
    return pl.BlockSpec((SEQ, 2 * DK), lambda h, s: (s, which * (H // 2) + h))


def attend_forward(qkv, bias, row, col):
    n = qkv.shape[0] // SEQ
    return pl.pallas_call(
        attend_kernel,
        grid=(H // 2, n),
        in_specs=[
            pair(0),
            pair(1),
            pair(2),
            pl.BlockSpec((2, SEQ, SEQ), lambda h, s: (h, 0, 0)),
            pl.BlockSpec((1, SEQ, 1), lambda h, s: (s, 0, 0)),
            pl.BlockSpec((1, 1, SEQ), lambda h, s: (s, 0, 0)),
        ],
        out_specs=[pl.BlockSpec((1, 2, SEQ, SEQ), lambda h, s: (s, h, 0, 0)), pair(0)],
        out_shape=[jax.ShapeDtypeStruct((n, H, SEQ, SEQ), bf16), jax.ShapeDtypeStruct((n * SEQ, H * DK), bf16)],
        cost_estimate=kernel_cost(0.5),
        name="attend_forward",
    )(qkv, qkv, qkv, bias, row, col)


def attend_back_kernel(q_ref, k_ref, v_ref, attend_ref, dctx_ref, dq_ref, dk_ref, dv_ref, skew_ref, ds_ref, skew_sum):
    keys = k_ref[...]
    values = v_ref[...]

    @pl.when(pl.program_id(1) == 0)
    def _():
        skew_sum[...] = jnp.zeros_like(skew_sum)

    for b in range(SEQ // RB):
        rows = pl.ds(b * RB, RB)
        start = SEQ - RB * b
        dq = None
        for side in range(2):
            p = attend_ref[0, side, rows].astype(f32)
            da = lax.dot_general(half_lanes(dctx_ref[rows], side), values, NT, preferred_element_type=f32)
            ds = (p * (da - jnp.sum(p * da, axis=-1, keepdims=True))).astype(bf16)
            ds_ref[side, rows] = ds
            part = half_lanes(jnp.dot(ds, keys, preferred_element_type=f32), side)
            dq = part if dq is None else dq + part
            skew_sum[side, :, start : start + SEQ] += ds.astype(f32)
        dq_ref[rows] = dq.astype(bf16)
    dk, dv = None, None
    for side in range(2):
        part = half_lanes(lax.dot_general(ds_ref[side], q_ref[...], TN, preferred_element_type=f32), side)
        dk = part if dk is None else dk + part
        part = half_lanes(lax.dot_general(attend_ref[0, side], dctx_ref[...], TN, preferred_element_type=f32), side)
        dv = part if dv is None else dv + part
    dk_ref[...] = dk.astype(bf16)
    dv_ref[...] = dv.astype(bf16)

    @pl.when(pl.program_id(1) == pl.num_programs(1) - 1)
    def _():
        for side in range(2):
            total = skew_sum[side, 0:8]
            for u in range(1, RB // 8):
                total += pltpu.roll(skew_sum[side, 8 * u : 8 * u + 8], 2 * SEQ - 8 * u, 1)
            row = lax.broadcasted_iota(jnp.int32, total.shape, 0)
            for bit in (1, 2, 4):
                total = jnp.where((row & bit) != 0, pltpu.roll(total, 2 * SEQ - bit, 1), total)
            skew_ref[side] = jnp.sum(total, axis=0, keepdims=True)


def attend_backward(qkv, attend, dctx):
    n = qkv.shape[0] // SEQ
    out = jax.ShapeDtypeStruct(dctx.shape, bf16)
    return pl.pallas_call(
        attend_back_kernel,
        grid=(H // 2, n),
        in_specs=[pair(0), pair(1), pair(2), pl.BlockSpec((1, 2, SEQ, SEQ), lambda h, s: (s, h, 0, 0)), pair(0)],
        out_specs=[pair(0), pair(0), pair(0), pl.BlockSpec((2, 1, 2 * SEQ), lambda h, s: (h, 0, 0))],
        out_shape=[out, out, out, jax.ShapeDtypeStruct((H, 1, 2 * SEQ), f32)],
        scratch_shapes=[pltpu.VMEM((2, SEQ, SEQ), bf16), pltpu.VMEM((2, RB, 2 * SEQ), f32)],
        cost_estimate=kernel_cost(22),
        name="attend_backward",
    )(qkv, qkv, qkv, attend, dctx)


class Copies:
    def __init__(self, sems):
        self.sems = sems; self.count = 0
    def start(self, src, dst):
        copy = pltpu.make_async_copy(src, dst, self.sems.at[self.count])
        self.count += 1
        copy.start()
        return copy

def wait(copies):
    for c in copies: c.wait()

def load_gate_up(copies, scal, wgu, own_gate, own_up, mine, other, groups):
    z, chunk, core = scal[0], scal[1], scal[2]
    block = own_gate.shape[1]
    started = []
    if other is None:
        for side in range(2):
            for at in range(groups):
                started.append(copies.start(mine.at[side, at], wgu.at[side, at * block : (at + 1) * block]))
        return started
    here = pl.ds(pl.multiple_of(z * block, 16), block)
    started.append(copies.start(own_gate.at[chunk], wgu.at[0, here]))
    started.append(copies.start(own_up.at[chunk], wgu.at[1, here]))
    for k in range(1, groups):
        at = lax.rem(z - k + groups, groups) * block
        for parts, side in ((mine, core), (other, 1 - core)):
            base = 0
            for part in parts:
                n = part.shape[1]
                started.append(copies.start(part.at[k - 1], wgu.at[side, pl.ds(pl.multiple_of(at + base, 8), n)]))
                base += n
    return started

def load_down(copies, scal, wd, own_down, mine, other, groups):
    z, chunk, core = scal[0], scal[1], scal[2]
    block = own_down.shape[1]
    if other is None:
        started = []
        half = block // 2
        for side in range(2):
            for at in range(groups):
                base = at * block + side * half
                started.append(copies.start(mine.at[side, at], wd.at[base : base + half]))
        return started
    started = [copies.start(own_down.at[chunk], wd.at[pl.ds(pl.multiple_of(z * block, 8), block)])]
    for k in range(1, groups):
        at = lax.rem(z - k + groups, groups) * block
        for parts, side in ((mine, core), (other, 1 - core)):
            base = at + side * (block // 2)
            for part in parts:
                n = part.shape[1]
                started.append(copies.start(part.at[k - 1], wd.at[pl.ds(pl.multiple_of(base, 8), n)]))
                base = base + n
    return started

def take_parts(it, n):
    if n == 0:
        return next(it), None
    return [next(it) for _ in range(n)], [next(it) for _ in range(n)]


def parts_of(source):
    if not isinstance(source, tuple):
        return 0, [source], source.shape[0] * source.shape[1]
    mine, other = source
    return len(mine), [*mine, *other], 2 + 2 * len(mine) * mine[0].shape[0]


def ffn_kernel(groups, nparts, *refs):
    it = iter(refs)
    scal = next(it); x_h, xt_h, g_h, own_gate, own_up, own_down = [next(it) for _ in range(6)]
    mine, other = take_parts(it, nparts[0])
    mine_d, other_d = take_parts(it, nparts[1])
    hid_h, dg_h, du_h, gm_h, go_h, gdm_h, gdo_h = [next(it) for _ in range(7)]
    x, xt, g, wgu, wd, hid, dga, dup, hidt, ggu, gd, sems = [next(it) for _ in range(12)]
    copies = Copies(sems)
    core = scal[2]
    c_x = copies.start(x_h, x)
    c_gu = load_gate_up(copies, scal, wgu, own_gate, own_up, mine, other, groups)
    c_g = copies.start(g_h, g)
    c_d = load_down(copies, scal, wd, own_down, mine_d, other_d, groups)
    c_xt = copies.start(xt_h, xt)
    tokens = x.shape[0]
    mb = MB
    c_x.wait()
    wait(c_gu)

    def gate_rows(m, _):
        rows = pl.ds(pl.multiple_of(m * mb, mb), mb)
        dga[rows] = jnp.dot(x[rows], wgu[0], preferred_element_type=f32).astype(bf16)
        return 0

    lax.fori_loop(0, tokens // mb, gate_rows, 0)
    c_g.wait()
    wait(c_d)

    def rows_step(m, _):
        rows = pl.ds(pl.multiple_of(m * mb, mb), mb)
        v = dga[rows].astype(f32)
        u = jnp.dot(x[rows], wgu[1], preferred_element_type=f32).astype(bf16).astype(f32)
        dh = lax.dot_general(g[rows], wd[...], NT, preferred_element_type=f32)
        sq = v * v
        half = 0.5 + 0.5 * jnp.tanh(v * (ROOT + (ROOT * CUBIC) * sq))
        act = v * half
        slope = half + (2.0 * v * half) * ((1.0 - half) * (ROOT + (3 * CUBIC * ROOT) * sq))
        h = (act * u).astype(bf16)
        hid[rows] = h
        dga[rows] = (dh * u * slope).astype(bf16)
        dup[rows] = (dh * act).astype(bf16)
        hidt[:, rows] = h.T
        return 0

    lax.fori_loop(0, tokens // mb, rows_step, 0)
    c_out = [copies.start(hid, hid_h), copies.start(dga, dg_h), copies.start(dup, du_h)]
    block = own_down.shape[1]
    half_block = block // 2
    def down_step(b, _):
        rows = pl.ds(pl.multiple_of(b * block, 16), block)
        gd[rows] = jnp.dot(hidt[rows], g[...], preferred_element_type=f32).astype(bf16)
        return 0
    lax.fori_loop(0, groups, down_step, 0)
    for b in range(groups):
        for side, dst in ((core, gdm_h), (1 - core, gdo_h)):
            c_out.append(copies.start(gd.at[pl.ds(pl.multiple_of(b * block + side * half_block, 8), half_block)], dst.at[b]))
    c_xt.wait()
    block = own_gate.shape[1]
    for i, act in ((0, dga), (1, dup)):
        def gate_step(b, _, i=i, act=act):
            rows = pl.ds(pl.multiple_of(b * block, 16), block)
            ggu[i, rows] = jnp.dot(xt[rows], act[...], preferred_element_type=f32).astype(bf16)
            return 0
        lax.fori_loop(0, groups, gate_step, 0)
        sem = sems.at[copies.count]
        copies.count += 1
        last = [pltpu.make_async_copy(ggu.at[i], dst, sem) for dst in (gm_h, go_h)]
        pl.when(core == i)(last[0].start)
        pl.when(core != i)(last[1].start)
        c_out.append(last[0])
    wait(c_out)


def ffn_chunk(scal, x, xt, g, own_gate, own_up, own_down, gate_up, down):
    tokens, d = x.shape
    groups = d // own_gate.shape[1]
    f = own_gate.shape[2]
    n_gu, arrays_gu, copies_gu = parts_of(gate_up)
    n_d, arrays_d, copies_d = parts_of(down)
    nparts = (n_gu, n_d)
    act = jax.ShapeDtypeStruct((tokens, f), bf16)
    gu = jax.ShapeDtypeStruct((d, f), bf16)
    gdn = jax.ShapeDtypeStruct((groups, own_down.shape[1] // 2, d), bf16)
    ins = [x, xt, g, own_gate, own_up, own_down, *arrays_gu, *arrays_d]
    ncop = 3 + copies_gu + copies_d + 3 + 2 * groups + 2
    V = lambda s: pltpu.VMEM(s, bf16)
    return pl.pallas_call(
        functools.partial(ffn_kernel, groups, nparts),
        in_specs=[pl.BlockSpec(memory_space=pltpu.SMEM)] + [ANY] * len(ins),
        out_specs=[ANY] * 7,
        out_shape=[act, act, act, gu, gu, gdn, gdn],
        scratch_shapes=[V((tokens, d)), V((d, tokens)), V((tokens, d)), V((2, d, f)), V((f, d)), V((tokens, f)), V((tokens, f)), V((tokens, f)), V((f, tokens)), V((2, d, f)), V((f, d)), pltpu.SemaphoreType.DMA((ncop,))],
        compiler_params=pltpu.CompilerParams(vmem_limit_bytes=VMEM_LIMIT),
        cost_estimate=kernel_cost(30),
        name="ffn_chunk",
    )(scal, *ins)

TB = 256


def norm_back_columns(values, gain, grad):
    r = lax.rsqrt(jnp.mean(values * values, axis=0, keepdims=True) + FLOOR)
    scaled = gain * grad
    back = r * scaled - values * ((r * r * r) * jnp.mean(scaled * values, axis=0, keepdims=True))
    return back, jnp.sum(grad * values * r, axis=1, keepdims=True)


def dx_kernel(groups, counts, *refs):
    it = iter(refs)
    scal = next(it)
    gain_h, middle_h, g_h = next(it), next(it), next(it)
    own_gate, own_up = next(it), next(it)
    chunks = []
    for n in counts:
        dg, du = next(it), next(it)
        chunks.append((dg, du, *take_parts(it, n)))
    dm_h, da_h, gg_h = next(it), next(it), next(it)
    acc, wgu, dga, dup, middle, g, gain, gg, sems = [next(it) for _ in range(9)]
    copies = Copies(sems)
    tokens = acc.shape[1]

    def load(j):
        dg, du, mine, other = chunks[j]
        s = (scal[0], scal[1] ^ j, scal[2])
        out = load_gate_up(copies, s, wgu.at[j % 2], own_gate, own_up, mine, other, groups)
        return out + [copies.start(dg, dga.at[j % 2]), copies.start(du, dup.at[j % 2])]

    pending = load(0)
    extra = [copies.start(gain_h, gain), copies.start(middle_h, middle), copies.start(g_h, g)]
    for j in range(len(chunks)):
        following = load(j + 1) if j + 1 < len(chunks) else []
        wait(pending)
        pending = following
        b = j % 2

        def step(m, _, j=j, b=b):
            at = pl.ds(pl.multiple_of(m * MB, MB), MB)
            part = lax.dot_general(wgu[b, 0], dga[b, at], NT, preferred_element_type=f32)
            part += lax.dot_general(wgu[b, 1], dup[b, at], NT, preferred_element_type=f32)
            acc[:, at] = part if j == 0 else acc[:, at] + part
            return 0

        lax.fori_loop(0, tokens // MB, step, 0)
    wait(extra)
    gg[...] = jnp.zeros_like(gg)

    def finish(m, _):
        at = pl.ds(pl.multiple_of(m * TB, TB), TB)
        back, part = norm_back_columns(middle[:, at], gain[...], acc[:, at])
        total = g[:, at].astype(f32) + back
        acc[:, at] = total
        g[:, at] = total.astype(bf16)
        gg[...] += part
        return 0

    lax.fori_loop(0, tokens // TB, finish, 0)
    wait([copies.start(g, da_h), copies.start(acc, dm_h), copies.start(gg, gg_h)])


def ffn_dx(scal, gain, middle_t, g_t, own_gate, own_up, chunks):
    tokens, f = chunks[0][0].shape
    d = middle_t.shape[0]
    groups = d // own_gate.shape[1]
    ins = [gain, middle_t, g_t, own_gate, own_up]
    ncop = 6
    counts = []
    for dg, du, source in chunks:
        n, arrays, copies = parts_of(source)
        counts.append(n)
        ins += [dg, du, *arrays]
        ncop += 2 + copies
    V = lambda s: pltpu.VMEM(s, bf16)
    F = lambda s: pltpu.VMEM(s, f32)
    return pl.pallas_call(
        functools.partial(dx_kernel, groups, tuple(counts)),
        in_specs=[pl.BlockSpec(memory_space=pltpu.SMEM)] + [ANY] * len(ins),
        out_specs=[ANY, ANY, ANY],
        out_shape=[jax.ShapeDtypeStruct((d, tokens), f32), jax.ShapeDtypeStruct((d, tokens), bf16), jax.ShapeDtypeStruct((d, 1), f32)],
        scratch_shapes=[F((d, tokens)), V((2, 2, d, f)), V((2, tokens, f)), V((2, tokens, f)), F((d, tokens)), V((d, tokens)), F((d, 1)), F((d, 1)), pltpu.SemaphoreType.DMA((ncop,))],
        compiler_params=pltpu.CompilerParams(vmem_limit_bytes=VMEM_LIMIT),
        cost_estimate=kernel_cost(35),
        name="ffn_dx",
    )(scal, *ins)


def middle_kernel(ctx_ref, w_ref, x_ref, gain_ref, mid_ref, nt_ref, n_ref):
    mid = x_ref[...].astype(f32) + lax.dot_general(w_ref[...], ctx_ref[...], NT, preferred_element_type=f32)
    mid_ref[...] = mid
    normed = mid * lax.rsqrt(jnp.mean(mid * mid, axis=0, keepdims=True) + FLOOR) * gain_ref[...]
    nt_ref[...] = normed.astype(bf16)
    n_ref[...] = normed.T.astype(bf16)


def middle_norm(context, wo_t, x_t, gain):
    d, tokens = x_t.shape
    width = context.shape[1]
    cols = pl.BlockSpec((d, TB), lambda i: (0, i))
    return pl.pallas_call(
        middle_kernel,
        grid=(tokens // TB,),
        in_specs=[pl.BlockSpec((TB, width), lambda i: (i, 0)), pl.BlockSpec((d, width), lambda i: (0, 0)), cols, pl.BlockSpec((d, 1), lambda i: (0, 0))],
        out_specs=[cols, cols, pl.BlockSpec((TB, d), lambda i: (i, 0))],
        out_shape=[jax.ShapeDtypeStruct((d, tokens), f32), jax.ShapeDtypeStruct((d, tokens), bf16), jax.ShapeDtypeStruct((tokens, d), bf16)],
        compiler_params=pltpu.CompilerParams(vmem_limit_bytes=VMEM_LIMIT),
        cost_estimate=kernel_cost(0.5),
        name="middle_norm",
    )(context, wo_t, x_t, gain)


def input_kernel(dq_ref, dk_ref, dv_ref, w_ref, x_ref, dm_ref, gain_ref, out_ref, gg_ref):
    grads = jnp.concatenate([dq_ref[...], dk_ref[...], dv_ref[...]], axis=1)
    d_normed = lax.dot_general(w_ref[...], grads, NT, preferred_element_type=f32)
    back, part = norm_back_columns(x_ref[...].astype(f32), gain_ref[...], d_normed)
    out_ref[...] = (dm_ref[...] + back).astype(bf16)

    @pl.when(pl.program_id(0) == 0)
    def _():
        gg_ref[...] = jnp.zeros_like(gg_ref)

    gg_ref[...] += part


def input_gradient(dq, dk, dv, wqkv, x_t, dm_t, gain):
    d, tokens = x_t.shape
    width = dq.shape[1]
    head = pl.BlockSpec((TB, width), lambda i: (i, 0))
    cols = pl.BlockSpec((d, TB), lambda i: (0, i))
    one = pl.BlockSpec((d, 1), lambda i: (0, 0))
    return pl.pallas_call(
        input_kernel,
        grid=(tokens // TB,),
        in_specs=[head, head, head, pl.BlockSpec((d, 3 * width), lambda i: (0, 0)), cols, cols, one],
        out_specs=[cols, one],
        out_shape=[jax.ShapeDtypeStruct((d, tokens), bf16), jax.ShapeDtypeStruct((d, 1), f32)],
        compiler_params=pltpu.CompilerParams(vmem_limit_bytes=VMEM_LIMIT),
        cost_estimate=kernel_cost(8),
        name="input_gradient",
    )(dq, dk, dv, wqkv, x_t, dm_t, gain)


def matrices_kernel(groups, *refs):
    scal, nt_h, dq_h, dk_h, dv_h, ctx_h, da_h, small_h, mine_h, other_h = refs[:10]
    nt, dqkv, ctx, ctx_t, da, small, buf, sems = refs[10:]
    d, tokens = nt.shape
    width = ctx.shape[1]
    rows = d // groups
    half = width // 2
    copies = Copies(sems)
    c_out = [copies.start(ctx_h, ctx), copies.start(da_h, da)]
    c_in = [copies.start(nt_h, nt), copies.start(small_h, small)]
    c_in += [copies.start(src, dqkv.at[m]) for m, src in enumerate((dq_h, dk_h, dv_h))]
    wait(c_out)
    ctx_t[...] = ctx[...].T
    grad_out = lax.dot_general(ctx_t[...], da[...], NT, preferred_element_type=f32).astype(bf16)
    n = width // groups
    for z in range(groups):
        for i in range(4):
            block = grad_out[z * n : (z + 1) * n, i * width : min(d, (i + 1) * width)]
            if block.shape[1] < width:
                block = jnp.concatenate([block, jnp.zeros((n, width - block.shape[1]), bf16)], axis=1)
            buf[i // 2, 3, z, (i % 2) * n : (i % 2 + 1) * n] = block
    wait(c_in)
    for m in range(3):

        def step(z, _, m=m):
            part = jnp.dot(nt[pl.ds(pl.multiple_of(z * rows, 16), rows)], dqkv[m], preferred_element_type=f32).astype(bf16)
            buf[0, m, z] = part[:half]
            buf[1, m, z, : rows - half] = part[half:]
            buf[1, m, z, rows - half :] = small[z]
            return 0

        lax.fori_loop(0, groups, step, 0)
    wait([copies.start(buf.at[scal[2]], mine_h), copies.start(buf.at[1 - scal[2]], other_h)])


def attention_matrices(scal, normed_t, dq, dk, dv, ctx, da_t, small):
    d, tokens = normed_t.shape
    groups = small.shape[0]
    width = dq.shape[1]
    out = jax.ShapeDtypeStruct((4, groups, width // 2, width), bf16)
    V = lambda s: pltpu.VMEM(s, bf16)
    return pl.pallas_call(
        functools.partial(matrices_kernel, groups),
        in_specs=[pl.BlockSpec(memory_space=pltpu.SMEM)] + [ANY] * 7,
        out_specs=[ANY, ANY],
        out_shape=[out, out],
        scratch_shapes=[V((d, tokens)), V((3, tokens, width)), V((tokens, width)), V((width, tokens)), V((d, tokens)), V(small.shape), V((2, *out.shape)), pltpu.SemaphoreType.DMA((9,))],
        compiler_params=pltpu.CompilerParams(vmem_limit_bytes=VMEM_LIMIT),
        cost_estimate=kernel_cost(9),
        name="attention_matrices",
    )(scal, normed_t, dq, dk, dv, ctx, da_t, small)


def out_kernel(groups, counts, *refs):
    it = iter(refs)
    scal = next(it)
    middle, own_down = next(it), next(it)
    chunks = []
    for n in counts:
        hid = next(it)
        chunks.append((hid, *take_parts(it, n)))
    out_h = next(it)
    acc, mid, out, wd, act, sems = [next(it) for _ in range(6)]
    copies = Copies(sems)

    def load(j):
        hid, mine, other = chunks[j]
        s = (scal[0], scal[1] ^ j, scal[2])
        return load_down(copies, s, wd.at[j % 2], own_down, mine, other, groups) + [copies.start(hid, act.at[j % 2])]

    c_middle = copies.start(middle, mid)
    pending = load(0)
    for j in range(len(chunks)):
        following = load(j + 1) if j + 1 < len(chunks) else []
        wait(pending)
        pending = following
        b = j % 2

        def step(m, _, j=j, b=b):
            rows = pl.ds(pl.multiple_of(m * MB, MB), MB)
            part = jnp.dot(act[b, rows], wd[b], preferred_element_type=f32)
            acc[rows] = part if j == 0 else acc[rows] + part
            return 0

        lax.fori_loop(0, acc.shape[0] // MB, step, 0)
    c_middle.wait()

    def finish(m, _):
        at = pl.ds(pl.multiple_of(m * TB, TB), TB)
        out[:, at] = (mid[:, at] + acc[at].T).astype(bf16)
        return 0

    lax.fori_loop(0, acc.shape[0] // TB, finish, 0)
    done = copies.start(out, out_h)
    done.wait()


def ffn_out(scal, middle, own_down, chunks):
    d, tokens = middle.shape
    f = chunks[0][0].shape[1]
    groups = f // own_down.shape[1]
    ins = [middle, own_down]
    ncop = 2
    counts = []
    for hid, source in chunks:
        n, arrays, copies = parts_of(source)
        counts.append(n)
        ins += [hid, *arrays]
        ncop += 1 + copies
    V = lambda s: pltpu.VMEM(s, bf16)
    return pl.pallas_call(
        functools.partial(out_kernel, groups, tuple(counts)),
        in_specs=[pl.BlockSpec(memory_space=pltpu.SMEM)] + [ANY] * len(ins),
        out_specs=ANY,
        out_shape=jax.ShapeDtypeStruct((d, tokens), bf16),
        scratch_shapes=[pltpu.VMEM((tokens, d), f32), pltpu.VMEM((d, tokens), f32), V((d, tokens)), V((2, f, d)), V((2, tokens, f)), pltpu.SemaphoreType.DMA((ncop,))],
        compiler_params=pltpu.CompilerParams(vmem_limit_bytes=VMEM_LIMIT),
        cost_estimate=kernel_cost(21),
        name="ffn_out",
    )(scal, *ins)


def split_kernel(gate_ref, up_ref, og_ref, ou_ref):
    quarter = og_ref.shape[0]
    width = og_ref.shape[2] // quarter
    for src, dst in ((gate_ref, og_ref), (up_ref, ou_ref)):
        for p in range(quarter):
            for b in range(quarter):
                at = (b * quarter + p) * width
                dst[p, :, b * width : (b + 1) * width] = src[:, at : at + width]


def split_columns(gate, up):
    rows, ff = gate.shape
    tile = rows // 2
    out = jax.ShapeDtypeStruct((4, rows, ff // 4), bf16)
    return pl.pallas_call(
        split_kernel,
        grid=(2,),
        in_specs=[pl.BlockSpec((tile, ff), lambda i: (i, 0))] * 2,
        out_specs=[pl.BlockSpec((4, tile, ff // 4), lambda i: (0, i, 0))] * 2,
        out_shape=[out, out],
        cost_estimate=kernel_cost(5),
        name="split_columns",
    )(gate, up)


def join_kernel(scal, *refs):
    mine, other, gate_ref, up_ref = refs
    me, core = scal[1], scal[2]
    width = mine.shape[2] // 4

    def put(p, j, side):
        for src, dst in ((mine, (gate_ref, up_ref)[side]), (other, (gate_ref, up_ref)[1 - side])):
            for b in range(4):
                at = (b * 4 + p) * width
                dst[:, at : at + width] = src[j, :, b * width : (b + 1) * width].astype(f32)

    for own in range(4):
        for side in range(2):

            @pl.when(jnp.logical_and(me == own, core == side))
            def _(own=own, side=side):
                for j in range(4):
                    put(own ^ j, j, side)


def join_columns(scal, mine, other):
    _, rows, f = mine.shape
    tile = rows // 2
    out = jax.ShapeDtypeStruct((rows, 4 * f), f32)
    return pl.pallas_call(
        join_kernel,
        grid=(2,),
        in_specs=[pl.BlockSpec(memory_space=pltpu.SMEM)] + [pl.BlockSpec((4, tile, f), lambda i: (0, i, 0))] * 2,
        out_specs=[pl.BlockSpec((tile, 4 * f), lambda i: (i, 0))] * 2,
        out_shape=[out, out],
        cost_estimate=kernel_cost(6.5),
        compiler_params=pltpu.CompilerParams(vmem_limit_bytes=VMEM_LIMIT),
        name="join_columns",
    )(scal, mine, other)


def weights_kernel(groups, *refs):
    scal = refs[0]
    mine, other = refs[1:5], refs[5:9]
    wqkv, wo, smalls, buf, flat, sems = refs[9:]
    rows = wqkv.shape[0] // groups
    width = buf.shape[-1]
    half = width // 2
    out_rows = width // groups
    d = wo.shape[0]
    copies = Copies(sems)
    done = []
    for j in range(4):
        for side, arrays in ((scal[2], mine), (1 - scal[2], other)):
            for k in range(groups):
                z = lax.rem(scal[0] - k + groups, groups)
                done.append(copies.start(arrays[j].at[k], buf.at[scal[1] ^ j, z, pl.ds(pl.multiple_of(side * half, 16), half)]))
    wait(done)
    for z in range(groups):
        for m in range(3):
            wqkv[z * rows : (z + 1) * rows, m * width : (m + 1) * width] = buf[m, z, :rows]
        for i in range(-(-d // width)):
            n = min(width, d - i * width)
            flat[z * out_rows : (z + 1) * out_rows, i * width : i * width + n] = buf[3, z, i * out_rows : (i + 1) * out_rows, :n]
        smalls[z] = buf[0, z, rows:]
    wo[...] = flat[...].T


def attention_weights(scal, mine, other, rows, d):
    groups, half, width = mine[0].shape
    V = pl.BlockSpec(memory_space=pltpu.VMEM)
    return pl.pallas_call(
        functools.partial(weights_kernel, groups),
        in_specs=[pl.BlockSpec(memory_space=pltpu.SMEM)] + [ANY] * 8,
        out_specs=[V, V, V],
        out_shape=[
            jax.ShapeDtypeStruct((groups * rows, 3 * width), bf16),
            jax.ShapeDtypeStruct((d, width), bf16),
            jax.ShapeDtypeStruct((groups, width - rows, width), bf16),
        ],
        scratch_shapes=[pltpu.VMEM((4, groups, width, width), bf16), pltpu.VMEM((width, d), bf16), pltpu.SemaphoreType.DMA((8 * groups,))],
        cost_estimate=kernel_cost(5.8),
        compiler_params=pltpu.CompilerParams(vmem_limit_bytes=VMEM_LIMIT),
        name="attention_weights",
    )(scal, *mine, *other)


def gradients_kernel(*refs):
    scal = refs[0]
    mine, other = refs[1:3]
    grads, grad_out, small, buf, sems = refs[3], refs[4], refs[5], refs[6], refs[7]
    rows = grads.shape[1]
    width = buf.shape[-1]
    half = width // 2
    out_rows, d = grad_out.shape
    copies = Copies(sems)
    done = []
    for j in range(4):
        for side, arrays in ((scal[2], mine), (1 - scal[2], other)):
            done.append(copies.start(arrays.at[j], buf.at[scal[1] ^ j, pl.ds(pl.multiple_of(side * half, 16), half)]))
    wait(done)
    for m in range(3):
        grads[m] = buf[m, :rows].astype(f32)
    for i in range(-(-d // width)):
        n = min(width, d - i * width)
        grad_out[:, i * width : i * width + n] = buf[3, i * out_rows : (i + 1) * out_rows, :n].astype(f32)
    small[...] = buf[0, rows:].astype(f32)


def attention_gradients(scal, mine, other, rows, out_rows, d):
    _, half, width = mine.shape
    V = pl.BlockSpec(memory_space=pltpu.VMEM)
    return pl.pallas_call(
        gradients_kernel,
        in_specs=[pl.BlockSpec(memory_space=pltpu.SMEM)] + [ANY] * 2,
        out_specs=[V, V, V],
        out_shape=[
            jax.ShapeDtypeStruct((3, rows, width), f32),
            jax.ShapeDtypeStruct((out_rows, d), f32),
            jax.ShapeDtypeStruct((width - rows, width), f32),
        ],
        scratch_shapes=[pltpu.VMEM((4, width, width), bf16), pltpu.SemaphoreType.DMA((8,))],
        cost_estimate=kernel_cost(3.5),
        compiler_params=pltpu.CompilerParams(vmem_limit_bytes=VMEM_LIMIT),
        name="attention_gradients",
    )(scal, mine, other)


def down_kernel(*refs):
    scal = refs[0]
    mine, other = refs[1:3]
    out, buf, sems = refs[3:]
    half = buf.shape[0] // 8
    copies = Copies(sems)
    done = []
    for j in range(4):
        for side, arrays in ((scal[2], mine), (1 - scal[2], other)):
            at = ((scal[1] ^ j) * 2 + side) * half
            done.append(copies.start(arrays.at[j], buf.at[pl.ds(pl.multiple_of(at, 16), half)]))
    wait(done)
    for i in range(buf.shape[0] // 128):
        rows = slice(i * 128, (i + 1) * 128)
        out[:, rows] = buf[rows].astype(f32).T


def down_gradient(scal, mine, other):
    _, half, d = mine.shape
    return pl.pallas_call(
        down_kernel,
        in_specs=[pl.BlockSpec(memory_space=pltpu.SMEM)] + [ANY] * 2,
        out_specs=pl.BlockSpec(memory_space=pltpu.VMEM),
        out_shape=jax.ShapeDtypeStruct((d, 8 * half), f32),
        scratch_shapes=[pltpu.VMEM((8 * half, d), bf16), pltpu.SemaphoreType.DMA((8,))],
        cost_estimate=kernel_cost(5.6),
        compiler_params=pltpu.CompilerParams(vmem_limit_bytes=VMEM_LIMIT),
        name="down_gradient",
    )(scal, mine, other)


def dot(left, right, form):
    return jnp.einsum(form, left, right, preferred_element_type=f32)


def add(*terms):
    total = terms[0].astype(f32)
    for term in terms[1:]:
        total = total + term.astype(f32)
    return total.astype(bf16)


def after(v, *others):
    return lax.optimization_barrier((v, others))[0]


def tie(*values):
    return lax.optimization_barrier(values)


def pick(stack, i):
    return lax.dynamic_index_in_dim(stack, i, 0, keepdims=False)


SHARD = ("outer", "chip", "core")


class Links:
    def __init__(self, shards, groups):
        self.shards, self.groups = shards, groups
        self.z = lax.axis_index("group")
        self.index = lax.axis_index(SHARD)
        self.core = self.index & 1
        self.chip = (self.index >> 1) & 3

    def swap(self, v, bit):
        return lax.ppermute(v, SHARD, [(i, i ^ bit) for i in range(self.shards)])

    def turn(self, v, k):
        return lax.ppermute(v, "group", [(i, (i + k) % self.groups) for i in range(self.groups)])

    def ring_gather(self, v):
        return [v] + [self.turn(v, k) for k in range(1, self.groups)]

    def others(self, v):
        return jnp.stack([pick(v, (self.z - k) % self.groups) for k in range(1, self.groups)])

    def ring_reduce(self, v, *others):
        at = lambda k: pick(v, (self.z + k) % self.groups)
        total = at(0).astype(f32)
        for k in range(1, self.groups):
            total = total + after(self.turn(at(k), k), *others).astype(f32)
        return total

    def beyond(self, total):
        bit = 8
        while bit < self.shards:
            total = total + self.swap(total, bit)
            bit *= 2
        return total


def local(
    layer_input_rows,
    gain_attn,
    w_query,
    w_key,
    w_value,
    w_out,
    gain_ff,
    gate_weight,
    w_up,
    w_down,
    bucket_head_bias,
    positions,
    rel_bucket,
    out_grad,
    *,
    shards,
    groups,
):
    links = Links(shards, groups)
    z, core, chip = links.z, links.core, links.chip
    tokens, d = layer_input_rows.shape
    seqs = tokens // SEQ
    width = w_query.shape[1]
    rows = w_query.shape[0]
    buckets = bucket_head_bias.shape[0] * groups
    scals = [jnp.stack([z, chip ^ j, core]).astype(jnp.int32) for j in range(4)]
    scal = scals[0]

    small = jnp.concatenate([gain_attn, gain_ff, bucket_head_bias.reshape(-1)])
    spare = width - rows
    small = jnp.pad(small, (0, spare * width - small.shape[0])).reshape(spare, width)
    out_blocks = -(-d // width)
    wo_block = jnp.pad(w_out, ((0, 0), (0, out_blocks * width - d)))
    wo_block = jnp.concatenate([wo_block[:, i * width : (i + 1) * width] for i in range(out_blocks)])
    tall = lambda w: jnp.concatenate([w, small])
    four = jnp.stack([tall(w_query), tall(w_key), tall(w_value), wo_block])
    half = width // 2
    piece = lax.dynamic_slice(four, (chip, core * half, 0), (1, half, width))[0]
    slots = links.ring_gather(piece)
    own_gate, own_up = split_columns(gate_weight, w_up)
    slots[1:] = after(slots[1:], own_gate)
    mine = [jnp.stack(slots)]
    x_t, g_t = layer_input_rows.T, out_grad.T
    g = lax.optimization_barrier(out_grad)
    arrived = [links.swap(mine[0], bit) for bit in (XBIT, YBIT, XBIT | YBIT)]
    mine += [after(a, g) for a in arrived]
    wqkv, wo_t, smalls = attention_weights(scal, mine, [links.swap(a, CORE) for a in mine], rows, d)
    smalls = smalls.reshape(groups, -1)
    gains = [smalls[:, i * rows : (i + 1) * rows].reshape(d, 1).astype(f32) for i in range(2)]
    bias_table = smalls[:, 2 * rows : 2 * rows + bucket_head_bias.size].reshape(buckets, H)

    own_down = w_down.reshape(4, -1, d)
    half_down = own_down.shape[1] // 2
    whole = lambda v: lax.all_gather(v, ("core", "group")).reshape(2, groups, *v.shape)
    gate_up_of = lambda p: jnp.where(core == 0, pick(own_gate, p), pick(own_up, p))
    down_of = lambda p: lax.dynamic_slice(own_down, (p, core * half_down, 0), (1, half_down, d))[0]
    near_gu = whole(after(gate_up_of(chip), *slots[1:]))

    inputs = x_t.astype(f32)
    r_attn = lax.rsqrt(jnp.mean(inputs * inputs, axis=0, keepdims=True) + FLOOR)
    normed_t = (inputs * r_attn * gains[0]).astype(bf16)
    qkv = dot(normed_t, wqkv, "dt,dc->tc").astype(bf16)
    onehot = (rel_bucket[:, None] == jnp.arange(buckets, dtype=jnp.int32)[None, :]).astype(f32)
    offsets = jnp.dot(onehot, bias_table.astype(f32), precision=lax.Precision.HIGHEST).T
    bias = bias_matrix(offsets[:, None, :])
    near_dn = whole(after(down_of(chip), bias))
    places = (positions // BLOCK).reshape(seqs, SEQ)
    bias, near_gu = tie(bias, near_gu)
    gu = links.others(pick(near_gu, core))
    gu_x, gu_y = links.swap(gu, XBIT), links.swap(gu, YBIT)
    attend, context = attend_forward(qkv, bias, places[:, :, None], places[:, None, :])
    middle_t, normed_ff_t, normed_ff = middle_norm(context, wo_t, x_t, gains[1])
    normed_ff, gu_x, gu_y = tie(normed_ff, gu_x, gu_y)
    dn = links.others(pick(after(near_dn, context), core))
    dn_x, dn_y = links.swap(dn, XBIT), links.swap(dn, YBIT)
    far_gu, far_dn = whole(after(gate_up_of(chip ^ 3), qkv)), whole(after(down_of(chip ^ 3), context))
    gus, dns = [near_gu], [near_dn]
    both = lambda parts: (parts, [links.swap(a, CORE) for a in parts])

    acts, sums_gu, sums_dn = [None] * 4, [None] * 4, [None] * 4

    def chunk(j, *deps):
        hid, dg, du, gm, go, dm, do = ffn_chunk(
            after(scals[j], *deps), normed_ff, normed_ff_t, g, own_gate, own_up, own_down, gus[j], dns[j]
        )
        acts[j] = (hid, dg, du)
        sums_gu[j] = add(gm, links.swap(go, CORE))
        sums_dn[j] = add(dm, links.swap(do, CORE))
        return hid

    scatter = lambda v: lax.psum_scatter(v, "group", scatter_dimension=0)
    done = chunk(0)
    gu_x, gu_y, dn_x, dn_y = after((gu_x, gu_y, dn_x, dn_y), done)
    gus += [both([gu_x]), both([gu_y])]
    dns += [both([dn_x]), both([dn_y])]
    gus.append(far_gu)
    dns.append(far_dn)
    rings = [None] * 4
    rings[0] = scatter(sums_dn[0])
    done = chunk(1, done, sums_dn[0], far_gu)
    rings[1] = scatter(sums_dn[1])
    done, rings[0] = tie(done, rings[0])
    done = chunk(2, done, sums_gu[0], sums_dn[1], far_dn)
    done, rings[1] = tie(done, rings[1])
    done = chunk(3, done, sums_gu[1], sums_dn[2])
    from_x, from_y = links.swap(sums_gu[1], XBIT), links.swap(sums_gu[2], YBIT)
    pair = scatter(jnp.stack([sums_dn[2], sums_dn[3]], axis=1))
    rings[2:] = pair[0], pair[1]
    far_sum = scatter(sums_gu[3].reshape(groups, rows, -1))
    d_middle_t, d_attn_t, grad_gain_ff = ffn_dx(
        after(scal, done, sums_gu[2], sums_gu[3], sums_dn[2], sums_dn[3]),
        gains[1],
        middle_t,
        g_t,
        own_gate,
        own_up,
        [(acts[j][1], acts[j][2], gus[j]) for j in range(4)],
    )
    d_context = dot(d_attn_t, wo_t, "dt,dc->tc").astype(bf16)
    d_context, from_x, from_y, *rings = tie(d_context, from_x, from_y, *rings)
    d_q, d_k, d_v, per_offset = attend_backward(qkv, attend, d_context)
    far = after([links.swap(rings[j], j << 1) for j in (1, 2, 3)], d_q)
    red_dn = rings[0].astype(f32)
    for part in far:
        red_dn = red_dn + part.astype(f32)
    red_dn = links.beyond(red_dn).astype(bf16)
    red_gu = scatter(add(sums_gu[0], from_x, from_y).reshape(groups, rows, -1))
    d_q, red_dn = tie(d_q, red_dn)
    grad_table = jnp.dot(onehot.T, per_offset[:, 0, :].T, precision=lax.Precision.HIGHEST)
    input_grad_t, grad_gain_attn = input_gradient(d_q, d_k, d_v, wqkv, x_t, d_middle_t, gains[0])

    def spread(v, *others):
        received = [after(links.swap(v, j << 1), *others) for j in (1, 2, 3)]
        mine = jnp.stack([v, *received])
        return mine, links.swap(mine, CORE)

    received = [links.swap(red_dn, j << 1) for j in (1, 2, 3)]
    input_grad_t, far_sum, *received = tie(input_grad_t, far_sum, *received)
    dn_mine = jnp.stack([red_dn, *received])
    dn_other = links.swap(dn_mine, CORE)
    far_sum = links.swap(far_sum, XBIT | YBIT)

    small = [grad_gain_attn.reshape(groups, -1), grad_gain_ff.reshape(groups, -1), grad_table.reshape(groups, -1)]
    small = jnp.concatenate(small, axis=1).astype(bf16)
    small = jnp.pad(small, ((0, 0), (0, spare * width - small.shape[1]))).reshape(groups, spare, width)
    mine, other = attention_matrices(after(scal, input_grad_t), normed_t, d_q, d_k, d_v, context, d_attn_t, small)
    mine, dn_other = tie(mine, dn_other)
    sums = add(mine, links.swap(other, CORE))
    output_t = ffn_out(after(scal, sums), middle_t, own_down, [(acts[j][0], dns[j]) for j in range(4)])
    plane = [links.swap(pick(sums, chip ^ j), j << 1) for j in (1, 2, 3)]
    output_t, far_sum, red_gu, *plane = tie(output_t, far_sum, red_gu, *plane)
    red_plane = add(pick(sums, chip), *plane)
    red_gu = links.beyond(red_gu.astype(f32) + far_sum.astype(f32)).astype(bf16)
    red_gu, red_plane = tie(red_gu, red_plane)
    red = scatter(red_plane)
    gu_x, gu_y = links.swap(red_gu, XBIT), links.swap(red_gu, YBIT)
    grad_down = down_gradient(scal, dn_mine, after(dn_other, red_gu)).T
    gu_x, gu_y, red, grad_down = tie(gu_x, gu_y, red, grad_down)
    mid = rows // 2
    gu_d = jnp.concatenate([links.swap(gu_x[:mid], YBIT), links.swap(gu_y[mid:], XBIT)])
    spread_gu = jnp.stack([red_gu, gu_x, gu_y, gu_d])
    grad_gate, grad_up = join_columns(scal, spread_gu, links.swap(spread_gu, CORE))
    wide, grad_out, small = attention_gradients(scal, *spread(links.beyond(red.astype(f32)).astype(bf16)), rows, *w_out.shape)
    small = small.reshape(-1)
    return (
        output_t.T,
        input_grad_t.T,
        small[:rows],
        wide[0],
        wide[1],
        wide[2],
        grad_out,
        small[rows : 2 * rows],
        grad_gate,
        grad_up,
        grad_down,
        small[2 * rows : 2 * rows + bucket_head_bias.size].reshape(bucket_head_bias.shape),
    )


def solution(mesh):
    shards, groups = mesh.shape["shard"], mesh.shape["group"]
    mesh = jax.sharding.Mesh(mesh.devices.reshape(shards // 8, 4, 2, groups), (*SHARD, "group"))
    split = P((*SHARD, "group"), None)
    rows = P("group", None)
    in_specs = (split, P("group"), rows, rows, rows, rows, P("group"), rows, rows, rows, rows, P((*SHARD, "group")), P(), split)
    out_specs = (split, split, P("group"), rows, rows, rows, rows, P("group"), rows, rows, rows, rows)
    body = functools.partial(local, shards=shards, groups=groups)
    return jax.shard_map(body, mesh=mesh, in_specs=in_specs, out_specs=out_specs, check_vma=False)
```

```python
import functools

import jax
import jax.numpy as jnp
from jax import lax
from jax.experimental import pallas as pl
from jax.experimental.pallas import tpu as pltpu
from jax.sharding import PartitionSpec as P

H = 6
DK = 64
SEQ = 512
BLOCK = 256
FLOOR = 1e-06
ROOT = 0.7978845608028654
CUBIC = 0.044715
RB = 256
RF = 256
MB = 512
VMEM_LIMIT = 60 << 20
NT = (((1,), (1,)), ((), ()))
TN = (((0,), (0,)), ((), ()))
ANY = pl.BlockSpec(memory_space=pl.ANY)
bf16 = jnp.bfloat16
f32 = jnp.float32
CORE, XBIT, YBIT = 1, 2, 4


def kernel_cost(us):
    return pl.CostEstimate(flops=int(us * 1.15e9), bytes_accessed=int(us * 1e6), transcendentals=0)


def skew_bias(off_ref, bias_ref):
    rows = jnp.broadcast_to(off_ref[0], (SEQ, 2 * SEQ))
    bias_ref[0] = pltpu.roll(rows, SEQ, 1, stride=1, stride_axis=0)[:, :SEQ].astype(bias_ref.dtype)


def bias_matrix(offsets):
    return pl.pallas_call(
        skew_bias,
        grid=(H,),
        in_specs=[pl.BlockSpec((1, 1, 2 * SEQ), lambda h: (h, 0, 0))],
        out_specs=pl.BlockSpec((1, SEQ, SEQ), lambda h: (h, 0, 0)),
        out_shape=jax.ShapeDtypeStruct((H, SEQ, SEQ), bf16),
        cost_estimate=kernel_cost(4),
        name="bias_matrix",
    )(offsets)


def half_lanes(v, side):
    lane = lax.broadcasted_iota(jnp.int32, v.shape, 1)
    return jnp.where((lane < DK) == (side == 0), v, jnp.zeros_like(v))


def attend_kernel(q_ref, k_ref, v_ref, bias_ref, row_ref, col_ref, attend_ref, ctx_ref):
    keys = k_ref[...]
    values = v_ref[...]
    col = col_ref[0]
    for b in range(SEQ // RF):
        rows = pl.ds(b * RF, RF)
        allowed = col <= row_ref[0, rows]
        ctx = None
        for side in range(2):
            s = lax.dot_general(half_lanes(q_ref[rows], side), keys, NT, preferred_element_type=f32)
            s = jnp.where(allowed, s + bias_ref[side, rows].astype(f32), -1e30)
            p = jnp.exp(s - jnp.max(s, axis=-1, keepdims=True))
            p = (p * (1.0 / jnp.sum(p, axis=-1, keepdims=True))).astype(bf16)
            attend_ref[0, side, rows] = p
            part = half_lanes(jnp.dot(p, values, preferred_element_type=f32), side)
            ctx = part if ctx is None else ctx + part
        ctx_ref[rows] = ctx.astype(bf16)


def pair(which):
    return pl.BlockSpec((SEQ, 2 * DK), lambda h, s: (s, which * (H // 2) + h))


def attend_forward(qkv, bias, row, col):
    n = qkv.shape[0] // SEQ
    return pl.pallas_call(
        attend_kernel,
        grid=(H // 2, n),
        in_specs=[
            pair(0),
            pair(1),
            pair(2),
            pl.BlockSpec((2, SEQ, SEQ), lambda h, s: (h, 0, 0)),
            pl.BlockSpec((1, SEQ, 1), lambda h, s: (s, 0, 0)),
            pl.BlockSpec((1, 1, SEQ), lambda h, s: (s, 0, 0)),
        ],
        out_specs=[pl.BlockSpec((1, 2, SEQ, SEQ), lambda h, s: (s, h, 0, 0)), pair(0)],
        out_shape=[jax.ShapeDtypeStruct((n, H, SEQ, SEQ), bf16), jax.ShapeDtypeStruct((n * SEQ, H * DK), bf16)],
        cost_estimate=kernel_cost(0.5),
        name="attend_forward",
    )(qkv, qkv, qkv, bias, row, col)


def attend_back_kernel(q_ref, k_ref, v_ref, attend_ref, dctx_ref, dq_ref, dk_ref, dv_ref, skew_ref, ds_ref, skew_sum):
    keys = k_ref[...]
    values = v_ref[...]

    @pl.when(pl.program_id(1) == 0)
    def _():
        skew_sum[...] = jnp.zeros_like(skew_sum)

    for b in range(SEQ // RB):
        rows = pl.ds(b * RB, RB)
        start = SEQ - RB * b
        dq = None
        for side in range(2):
            p = attend_ref[0, side, rows].astype(f32)
            da = lax.dot_general(half_lanes(dctx_ref[rows], side), values, NT, preferred_element_type=f32)
            ds = (p * (da - jnp.sum(p * da, axis=-1, keepdims=True))).astype(bf16)
            ds_ref[side, rows] = ds
            part = half_lanes(jnp.dot(ds, keys, preferred_element_type=f32), side)
            dq = part if dq is None else dq + part
            skew_sum[side, :, start : start + SEQ] += ds.astype(f32)
        dq_ref[rows] = dq.astype(bf16)
    dk, dv = None, None
    for side in range(2):
        part = half_lanes(lax.dot_general(ds_ref[side], q_ref[...], TN, preferred_element_type=f32), side)
        dk = part if dk is None else dk + part
        part = half_lanes(lax.dot_general(attend_ref[0, side], dctx_ref[...], TN, preferred_element_type=f32), side)
        dv = part if dv is None else dv + part
    dk_ref[...] = dk.astype(bf16)
    dv_ref[...] = dv.astype(bf16)

    @pl.when(pl.program_id(1) == pl.num_programs(1) - 1)
    def _():
        for side in range(2):
            total = skew_sum[side, 0:8]
            for u in range(1, RB // 8):
                total += pltpu.roll(skew_sum[side, 8 * u : 8 * u + 8], 2 * SEQ - 8 * u, 1)
            row = lax.broadcasted_iota(jnp.int32, total.shape, 0)
            for bit in (1, 2, 4):
                total = jnp.where((row & bit) != 0, pltpu.roll(total, 2 * SEQ - bit, 1), total)
            skew_ref[side] = jnp.sum(total, axis=0, keepdims=True)


def attend_backward(qkv, attend, dctx):
    n = qkv.shape[0] // SEQ
    out = jax.ShapeDtypeStruct(dctx.shape, bf16)
    return pl.pallas_call(
        attend_back_kernel,
        grid=(H // 2, n),
        in_specs=[pair(0), pair(1), pair(2), pl.BlockSpec((1, 2, SEQ, SEQ), lambda h, s: (s, h, 0, 0)), pair(0)],
        out_specs=[pair(0), pair(0), pair(0), pl.BlockSpec((2, 1, 2 * SEQ), lambda h, s: (h, 0, 0))],
        out_shape=[out, out, out, jax.ShapeDtypeStruct((H, 1, 2 * SEQ), f32)],
        scratch_shapes=[pltpu.VMEM((2, SEQ, SEQ), bf16), pltpu.VMEM((2, RB, 2 * SEQ), f32)],
        cost_estimate=kernel_cost(22),
        name="attend_backward",
    )(qkv, qkv, qkv, attend, dctx)


class Copies:
    def __init__(self, sems):
        self.sems = sems; self.count = 0
    def start(self, src, dst):
        copy = pltpu.make_async_copy(src, dst, self.sems.at[self.count])
        self.count += 1
        copy.start()
        return copy

def wait(copies):
    for c in copies: c.wait()

def load_gate_up(copies, scal, wgu, own_gate, own_up, mine, other, groups):
    z, chunk, core = scal[0], scal[1], scal[2]
    block = own_gate.shape[1]
    started = []
    if other is None:
        for side in range(2):
            for at in range(groups):
                started.append(copies.start(mine.at[side, at], wgu.at[side, at * block : (at + 1) * block]))
        return started
    here = pl.ds(pl.multiple_of(z * block, 16), block)
    started.append(copies.start(own_gate.at[chunk], wgu.at[0, here]))
    started.append(copies.start(own_up.at[chunk], wgu.at[1, here]))
    for k in range(1, groups):
        at = lax.rem(z - k + groups, groups) * block
        for parts, side in ((mine, core), (other, 1 - core)):
            base = 0
            for part in parts:
                n = part.shape[1]
                started.append(copies.start(part.at[k - 1], wgu.at[side, pl.ds(pl.multiple_of(at + base, 8), n)]))
                base += n
    return started

def load_down(copies, scal, wd, own_down, mine, other, groups):
    z, chunk, core = scal[0], scal[1], scal[2]
    block = own_down.shape[1]
    if other is None:
        started = []
        half = block // 2
        for side in range(2):
            for at in range(groups):
                base = at * block + side * half
                started.append(copies.start(mine.at[side, at], wd.at[base : base + half]))
        return started
    started = [copies.start(own_down.at[chunk], wd.at[pl.ds(pl.multiple_of(z * block, 8), block)])]
    for k in range(1, groups):
        at = lax.rem(z - k + groups, groups) * block
        for parts, side in ((mine, core), (other, 1 - core)):
            base = at + side * (block // 2)
            for part in parts:
                n = part.shape[1]
                started.append(copies.start(part.at[k - 1], wd.at[pl.ds(pl.multiple_of(base, 8), n)]))
                base = base + n
    return started

def take_parts(it, n):
    if n == 0:
        return next(it), None
    return [next(it) for _ in range(n)], [next(it) for _ in range(n)]


def parts_of(source):
    if not isinstance(source, tuple):
        return 0, [source], source.shape[0] * source.shape[1]
    mine, other = source
    return len(mine), [*mine, *other], 2 + 2 * len(mine) * mine[0].shape[0]


def ffn_kernel(groups, nparts, *refs):
    it = iter(refs)
    scal = next(it); x_h, xt_h, g_h, own_gate, own_up, own_down = [next(it) for _ in range(6)]
    mine, other = take_parts(it, nparts[0])
    mine_d, other_d = take_parts(it, nparts[1])
    hid_h, dg_h, du_h, gm_h, go_h, gdm_h, gdo_h = [next(it) for _ in range(7)]
    x, xt, g, wgu, wd, hid, dga, dup, hidt, ggu, gd, sems = [next(it) for _ in range(12)]
    copies = Copies(sems)
    core = scal[2]
    c_x = copies.start(x_h, x)
    c_gu = load_gate_up(copies, scal, wgu, own_gate, own_up, mine, other, groups)
    c_g = copies.start(g_h, g)
    c_d = load_down(copies, scal, wd, own_down, mine_d, other_d, groups)
    c_xt = copies.start(xt_h, xt)
    tokens = x.shape[0]
    mb = 256
    c_x.wait()
    wait(c_gu)

    def gate_rows(m, _):
        rows = pl.ds(pl.multiple_of(m * mb, mb), mb)
        dga[rows] = jnp.dot(x[rows], wgu[0], preferred_element_type=f32).astype(bf16)
        return 0

    lax.fori_loop(0, tokens // mb, gate_rows, 0)
    c_g.wait()
    wait(c_d)

    def rows_step(m, _):
        rows = pl.ds(pl.multiple_of(m * mb, mb), mb)
        v = dga[rows].astype(f32)
        u = jnp.dot(x[rows], wgu[1], preferred_element_type=f32).astype(bf16).astype(f32)
        dh = lax.dot_general(g[rows], wd[...], NT, preferred_element_type=f32)
        sq = v * v
        half = 0.5 + 0.5 * jnp.tanh(v * (ROOT + (ROOT * CUBIC) * sq))
        act = v * half
        slope = half + (2.0 * v * half) * ((1.0 - half) * (ROOT + (3 * CUBIC * ROOT) * sq))
        h = (act * u).astype(bf16)
        hid[rows] = h
        dga[rows] = (dh * u * slope).astype(bf16)
        dup[rows] = (dh * act).astype(bf16)
        hidt[:, rows] = h.T
        return 0

    lax.fori_loop(0, tokens // mb, rows_step, 0)
    c_out = [copies.start(hid, hid_h), copies.start(dga, dg_h), copies.start(dup, du_h)]
    block = own_down.shape[1]
    half_block = block // 2
    def down_step(b, _):
        rows = pl.ds(pl.multiple_of(b * block, 16), block)
        gd[rows] = jnp.dot(hidt[rows], g[...], preferred_element_type=f32).astype(bf16)
        return 0
    lax.fori_loop(0, groups, down_step, 0)
    for b in range(groups):
        for side, dst in ((core, gdm_h), (1 - core, gdo_h)):
            c_out.append(copies.start(gd.at[pl.ds(pl.multiple_of(b * block + side * half_block, 8), half_block)], dst.at[b]))
    c_xt.wait()
    block = own_gate.shape[1]
    for i, act in ((0, dga), (1, dup)):
        def gate_step(b, _, i=i, act=act):
            rows = pl.ds(pl.multiple_of(b * block, 16), block)
            ggu[i, rows] = jnp.dot(xt[rows], act[...], preferred_element_type=f32).astype(bf16)
            return 0
        lax.fori_loop(0, groups, gate_step, 0)
        sem = sems.at[copies.count]
        copies.count += 1
        last = [pltpu.make_async_copy(ggu.at[i], dst, sem) for dst in (gm_h, go_h)]
        pl.when(core == i)(last[0].start)
        pl.when(core != i)(last[1].start)
        c_out.append(last[0])
    wait(c_out)


def ffn_chunk(scal, x, xt, g, own_gate, own_up, own_down, gate_up, down):
    tokens, d = x.shape
    groups = d // own_gate.shape[1]
    f = own_gate.shape[2]
    n_gu, arrays_gu, copies_gu = parts_of(gate_up)
    n_d, arrays_d, copies_d = parts_of(down)
    nparts = (n_gu, n_d)
    act = jax.ShapeDtypeStruct((tokens, f), bf16)
    gu = jax.ShapeDtypeStruct((d, f), bf16)
    gdn = jax.ShapeDtypeStruct((groups, own_down.shape[1] // 2, d), bf16)
    ins = [x, xt, g, own_gate, own_up, own_down, *arrays_gu, *arrays_d]
    ncop = 3 + copies_gu + copies_d + 3 + 2 * groups + 2
    V = lambda s: pltpu.VMEM(s, bf16)
    return pl.pallas_call(
        functools.partial(ffn_kernel, groups, nparts),
        in_specs=[pl.BlockSpec(memory_space=pltpu.SMEM)] + [ANY] * len(ins),
        out_specs=[ANY] * 7,
        out_shape=[act, act, act, gu, gu, gdn, gdn],
        scratch_shapes=[V((tokens, d)), V((d, tokens)), V((tokens, d)), V((2, d, f)), V((f, d)), V((tokens, f)), V((tokens, f)), V((tokens, f)), V((f, tokens)), V((2, d, f)), V((f, d)), pltpu.SemaphoreType.DMA((ncop,))],
        compiler_params=pltpu.CompilerParams(vmem_limit_bytes=VMEM_LIMIT),
        cost_estimate=kernel_cost(30),
        name="ffn_chunk",
    )(scal, *ins)

TB = 256


def norm_back_columns(values, gain, grad):
    r = lax.rsqrt(jnp.mean(values * values, axis=0, keepdims=True) + FLOOR)
    scaled = gain * grad
    back = r * scaled - values * ((r * r * r) * jnp.mean(scaled * values, axis=0, keepdims=True))
    return back, jnp.sum(grad * values * r, axis=1, keepdims=True)


def dx_kernel(groups, counts, *refs):
    it = iter(refs)
    scal = next(it)
    gain_h, middle_h, g_h = next(it), next(it), next(it)
    own_gate, own_up = next(it), next(it)
    chunks = []
    for n in counts:
        dg, du = next(it), next(it)
        chunks.append((dg, du, *take_parts(it, n)))
    dm_h, da_h, gg_h = next(it), next(it), next(it)
    acc, wgu, dga, dup, middle, g, gain, gg, sems = [next(it) for _ in range(9)]
    copies = Copies(sems)
    tokens = acc.shape[1]

    def load(j):
        dg, du, mine, other = chunks[j]
        s = (scal[0], scal[1] ^ j, scal[2])
        out = load_gate_up(copies, s, wgu.at[j % 2], own_gate, own_up, mine, other, groups)
        return out + [copies.start(dg, dga.at[j % 2]), copies.start(du, dup.at[j % 2])]

    pending = load(0)
    extra = [copies.start(gain_h, gain), copies.start(middle_h, middle), copies.start(g_h, g)]
    for j in range(len(chunks)):
        following = load(j + 1) if j + 1 < len(chunks) else []
        wait(pending)
        pending = following
        b = j % 2

        def step(m, _, j=j, b=b):
            at = pl.ds(pl.multiple_of(m * MB, MB), MB)
            part = lax.dot_general(wgu[b, 0], dga[b, at], NT, preferred_element_type=f32)
            part += lax.dot_general(wgu[b, 1], dup[b, at], NT, preferred_element_type=f32)
            acc[:, at] = part if j == 0 else acc[:, at] + part
            return 0

        lax.fori_loop(0, tokens // MB, step, 0)
    wait(extra)
    gg[...] = jnp.zeros_like(gg)

    def finish(m, _):
        at = pl.ds(pl.multiple_of(m * MB, MB), MB)
        back, part = norm_back_columns(middle[:, at], gain[...], acc[:, at])
        total = g[:, at].astype(f32) + back
        acc[:, at] = total
        g[:, at] = total.astype(bf16)
        gg[...] += part
        return 0

    lax.fori_loop(0, tokens // MB, finish, 0)
    wait([copies.start(g, da_h), copies.start(acc, dm_h), copies.start(gg, gg_h)])


def ffn_dx(scal, gain, middle_t, g_t, own_gate, own_up, chunks):
    tokens, f = chunks[0][0].shape
    d = middle_t.shape[0]
    groups = d // own_gate.shape[1]
    ins = [gain, middle_t, g_t, own_gate, own_up]
    ncop = 6
    counts = []
    for dg, du, source in chunks:
        n, arrays, copies = parts_of(source)
        counts.append(n)
        ins += [dg, du, *arrays]
        ncop += 2 + copies
    V = lambda s: pltpu.VMEM(s, bf16)
    F = lambda s: pltpu.VMEM(s, f32)
    return pl.pallas_call(
        functools.partial(dx_kernel, groups, tuple(counts)),
        in_specs=[pl.BlockSpec(memory_space=pltpu.SMEM)] + [ANY] * len(ins),
        out_specs=[ANY, ANY, ANY],
        out_shape=[jax.ShapeDtypeStruct((d, tokens), f32), jax.ShapeDtypeStruct((d, tokens), bf16), jax.ShapeDtypeStruct((d, 1), f32)],
        scratch_shapes=[F((d, tokens)), V((2, 2, d, f)), V((2, tokens, f)), V((2, tokens, f)), F((d, tokens)), V((d, tokens)), F((d, 1)), F((d, 1)), pltpu.SemaphoreType.DMA((ncop,))],
        compiler_params=pltpu.CompilerParams(vmem_limit_bytes=VMEM_LIMIT),
        cost_estimate=kernel_cost(35),
        name="ffn_dx",
    )(scal, *ins)


def middle_kernel(ctx_ref, w_ref, x_ref, gain_ref, mid_ref, nt_ref, n_ref):
    mid = x_ref[...].astype(f32) + lax.dot_general(w_ref[...], ctx_ref[...], NT, preferred_element_type=f32)
    mid_ref[...] = mid
    normed = mid * lax.rsqrt(jnp.mean(mid * mid, axis=0, keepdims=True) + FLOOR) * gain_ref[...]
    nt_ref[...] = normed.astype(bf16)
    n_ref[...] = normed.T.astype(bf16)


def middle_norm(context, wo_t, x_t, gain):
    d, tokens = x_t.shape
    width = context.shape[1]
    cols = pl.BlockSpec((d, TB), lambda i: (0, i))
    return pl.pallas_call(
        middle_kernel,
        grid=(tokens // TB,),
        in_specs=[pl.BlockSpec((TB, width), lambda i: (i, 0)), pl.BlockSpec((d, width), lambda i: (0, 0)), cols, pl.BlockSpec((d, 1), lambda i: (0, 0))],
        out_specs=[cols, cols, pl.BlockSpec((TB, d), lambda i: (i, 0))],
        out_shape=[jax.ShapeDtypeStruct((d, tokens), f32), jax.ShapeDtypeStruct((d, tokens), bf16), jax.ShapeDtypeStruct((tokens, d), bf16)],
        compiler_params=pltpu.CompilerParams(vmem_limit_bytes=VMEM_LIMIT),
        cost_estimate=kernel_cost(0.5),
        name="middle_norm",
    )(context, wo_t, x_t, gain)


def input_kernel(dq_ref, dk_ref, dv_ref, w_ref, x_ref, dm_ref, gain_ref, out_ref, gg_ref):
    grads = jnp.concatenate([dq_ref[...], dk_ref[...], dv_ref[...]], axis=1)
    d_normed = lax.dot_general(w_ref[...], grads, NT, preferred_element_type=f32)
    back, part = norm_back_columns(x_ref[...].astype(f32), gain_ref[...], d_normed)
    out_ref[...] = (dm_ref[...] + back).astype(bf16)

    @pl.when(pl.program_id(0) == 0)
    def _():
        gg_ref[...] = jnp.zeros_like(gg_ref)

    gg_ref[...] += part


def input_gradient(dq, dk, dv, wqkv, x_t, dm_t, gain):
    d, tokens = x_t.shape
    width = dq.shape[1]
    head = pl.BlockSpec((TB, width), lambda i: (i, 0))
    cols = pl.BlockSpec((d, TB), lambda i: (0, i))
    one = pl.BlockSpec((d, 1), lambda i: (0, 0))
    return pl.pallas_call(
        input_kernel,
        grid=(tokens // TB,),
        in_specs=[head, head, head, pl.BlockSpec((d, 3 * width), lambda i: (0, 0)), cols, cols, one],
        out_specs=[cols, one],
        out_shape=[jax.ShapeDtypeStruct((d, tokens), bf16), jax.ShapeDtypeStruct((d, 1), f32)],
        compiler_params=pltpu.CompilerParams(vmem_limit_bytes=VMEM_LIMIT),
        cost_estimate=kernel_cost(8),
        name="input_gradient",
    )(dq, dk, dv, wqkv, x_t, dm_t, gain)


def matrices_kernel(groups, *refs):
    scal, nt_h, dq_h, dk_h, dv_h, ctx_h, da_h, small_h, mine_h, other_h = refs[:10]
    nt, dqkv, ctx, ctx_t, da, small, buf, sems = refs[10:]
    d, tokens = nt.shape
    width = ctx.shape[1]
    rows = d // groups
    half = width // 2
    copies = Copies(sems)
    c_out = [copies.start(ctx_h, ctx), copies.start(da_h, da)]
    c_in = [copies.start(nt_h, nt), copies.start(small_h, small)]
    c_in += [copies.start(src, dqkv.at[m]) for m, src in enumerate((dq_h, dk_h, dv_h))]
    wait(c_out)
    ctx_t[...] = ctx[...].T
    grad_out = lax.dot_general(ctx_t[...], da[...], NT, preferred_element_type=f32).astype(bf16)
    n = width // groups
    for z in range(groups):
        for i in range(4):
            block = grad_out[z * n : (z + 1) * n, i * width : min(d, (i + 1) * width)]
            if block.shape[1] < width:
                block = jnp.concatenate([block, jnp.zeros((n, width - block.shape[1]), bf16)], axis=1)
            buf[i // 2, 3, z, (i % 2) * n : (i % 2 + 1) * n] = block
    wait(c_in)
    for m in range(3):

        def step(z, _, m=m):
            part = jnp.dot(nt[pl.ds(pl.multiple_of(z * rows, 16), rows)], dqkv[m], preferred_element_type=f32).astype(bf16)
            buf[0, m, z] = part[:half]
            buf[1, m, z, : rows - half] = part[half:]
            buf[1, m, z, rows - half :] = small[z]
            return 0

        lax.fori_loop(0, groups, step, 0)
    wait([copies.start(buf.at[scal[2]], mine_h), copies.start(buf.at[1 - scal[2]], other_h)])


def attention_matrices(scal, normed_t, dq, dk, dv, ctx, da_t, small):
    d, tokens = normed_t.shape
    groups = small.shape[0]
    width = dq.shape[1]
    out = jax.ShapeDtypeStruct((4, groups, width // 2, width), bf16)
    V = lambda s: pltpu.VMEM(s, bf16)
    return pl.pallas_call(
        functools.partial(matrices_kernel, groups),
        in_specs=[pl.BlockSpec(memory_space=pltpu.SMEM)] + [ANY] * 7,
        out_specs=[ANY, ANY],
        out_shape=[out, out],
        scratch_shapes=[V((d, tokens)), V((3, tokens, width)), V((tokens, width)), V((width, tokens)), V((d, tokens)), V(small.shape), V((2, *out.shape)), pltpu.SemaphoreType.DMA((9,))],
        compiler_params=pltpu.CompilerParams(vmem_limit_bytes=VMEM_LIMIT),
        cost_estimate=kernel_cost(9),
        name="attention_matrices",
    )(scal, normed_t, dq, dk, dv, ctx, da_t, small)


def out_kernel(groups, counts, *refs):
    it = iter(refs)
    scal = next(it)
    middle, own_down = next(it), next(it)
    chunks = []
    for n in counts:
        hid = next(it)
        chunks.append((hid, *take_parts(it, n)))
    out_h = next(it)
    acc, mid, out, wd, act, sems = [next(it) for _ in range(6)]
    copies = Copies(sems)

    def load(j):
        hid, mine, other = chunks[j]
        s = (scal[0], scal[1] ^ j, scal[2])
        return load_down(copies, s, wd.at[j % 2], own_down, mine, other, groups) + [copies.start(hid, act.at[j % 2])]

    c_middle = copies.start(middle, mid)
    pending = load(0)
    for j in range(len(chunks)):
        following = load(j + 1) if j + 1 < len(chunks) else []
        wait(pending)
        pending = following
        b = j % 2

        def step(m, _, j=j, b=b):
            rows = pl.ds(pl.multiple_of(m * MB, MB), MB)
            part = jnp.dot(act[b, rows], wd[b], preferred_element_type=f32)
            acc[rows] = part if j == 0 else acc[rows] + part
            return 0

        lax.fori_loop(0, acc.shape[0] // MB, step, 0)
    c_middle.wait()

    def finish(m, _):
        at = pl.ds(pl.multiple_of(m * TB, TB), TB)
        out[:, at] = (mid[:, at] + acc[at].T).astype(bf16)
        return 0

    lax.fori_loop(0, acc.shape[0] // TB, finish, 0)
    done = copies.start(out, out_h)
    done.wait()


def ffn_out(scal, middle, own_down, chunks):
    d, tokens = middle.shape
    f = chunks[0][0].shape[1]
    groups = f // own_down.shape[1]
    ins = [middle, own_down]
    ncop = 2
    counts = []
    for hid, source in chunks:
        n, arrays, copies = parts_of(source)
        counts.append(n)
        ins += [hid, *arrays]
        ncop += 1 + copies
    V = lambda s: pltpu.VMEM(s, bf16)
    return pl.pallas_call(
        functools.partial(out_kernel, groups, tuple(counts)),
        in_specs=[pl.BlockSpec(memory_space=pltpu.SMEM)] + [ANY] * len(ins),
        out_specs=ANY,
        out_shape=jax.ShapeDtypeStruct((d, tokens), bf16),
        scratch_shapes=[pltpu.VMEM((tokens, d), f32), pltpu.VMEM((d, tokens), f32), V((d, tokens)), V((2, f, d)), V((2, tokens, f)), pltpu.SemaphoreType.DMA((ncop,))],
        compiler_params=pltpu.CompilerParams(vmem_limit_bytes=VMEM_LIMIT),
        cost_estimate=kernel_cost(21),
        name="ffn_out",
    )(scal, *ins)


def split_kernel(gate_ref, up_ref, og_ref, ou_ref):
    quarter = og_ref.shape[0]
    width = og_ref.shape[2] // quarter
    for src, dst in ((gate_ref, og_ref), (up_ref, ou_ref)):
        for p in range(quarter):
            for b in range(quarter):
                at = (b * quarter + p) * width
                dst[p, :, b * width : (b + 1) * width] = src[:, at : at + width]


def split_columns(gate, up):
    rows, ff = gate.shape
    tile = rows // 2
    out = jax.ShapeDtypeStruct((4, rows, ff // 4), bf16)
    return pl.pallas_call(
        split_kernel,
        grid=(2,),
        in_specs=[pl.BlockSpec((tile, ff), lambda i: (i, 0))] * 2,
        out_specs=[pl.BlockSpec((4, tile, ff // 4), lambda i: (0, i, 0))] * 2,
        out_shape=[out, out],
        cost_estimate=kernel_cost(5),
        name="split_columns",
    )(gate, up)


def join_kernel(scal, *refs):
    mine, other, gate_ref, up_ref = refs
    me, core = scal[1], scal[2]
    width = mine.shape[2] // 4

    def put(p, j, side):
        for src, dst in ((mine, (gate_ref, up_ref)[side]), (other, (gate_ref, up_ref)[1 - side])):
            for b in range(4):
                at = (b * 4 + p) * width
                dst[:, at : at + width] = src[j, :, b * width : (b + 1) * width].astype(f32)

    for own in range(4):
        for side in range(2):

            @pl.when(jnp.logical_and(me == own, core == side))
            def _(own=own, side=side):
                for j in range(4):
                    put(own ^ j, j, side)


def join_columns(scal, mine, other):
    _, rows, f = mine.shape
    tile = rows // 2
    out = jax.ShapeDtypeStruct((rows, 4 * f), f32)
    return pl.pallas_call(
        join_kernel,
        grid=(2,),
        in_specs=[pl.BlockSpec(memory_space=pltpu.SMEM)] + [pl.BlockSpec((4, tile, f), lambda i: (0, i, 0))] * 2,
        out_specs=[pl.BlockSpec((tile, 4 * f), lambda i: (i, 0))] * 2,
        out_shape=[out, out],
        cost_estimate=kernel_cost(6.5),
        compiler_params=pltpu.CompilerParams(vmem_limit_bytes=VMEM_LIMIT),
        name="join_columns",
    )(scal, mine, other)


def weights_kernel(groups, *refs):
    scal = refs[0]
    mine, other = refs[1:5], refs[5:9]
    wqkv, wo, smalls, buf, flat, sems = refs[9:]
    rows = wqkv.shape[0] // groups
    width = buf.shape[-1]
    half = width // 2
    out_rows = width // groups
    d = wo.shape[0]
    copies = Copies(sems)
    done = []
    for j in range(4):
        for side, arrays in ((scal[2], mine), (1 - scal[2], other)):
            for k in range(groups):
                z = lax.rem(scal[0] - k + groups, groups)
                done.append(copies.start(arrays[j].at[k], buf.at[scal[1] ^ j, z, pl.ds(pl.multiple_of(side * half, 16), half)]))
    wait(done)
    for z in range(groups):
        for m in range(3):
            wqkv[z * rows : (z + 1) * rows, m * width : (m + 1) * width] = buf[m, z, :rows]
        for i in range(-(-d // width)):
            n = min(width, d - i * width)
            flat[z * out_rows : (z + 1) * out_rows, i * width : i * width + n] = buf[3, z, i * out_rows : (i + 1) * out_rows, :n]
        smalls[z] = buf[0, z, rows:]
    wo[...] = flat[...].T


def attention_weights(scal, mine, other, rows, d):
    groups, half, width = mine[0].shape
    V = pl.BlockSpec(memory_space=pltpu.VMEM)
    return pl.pallas_call(
        functools.partial(weights_kernel, groups),
        in_specs=[pl.BlockSpec(memory_space=pltpu.SMEM)] + [ANY] * 8,
        out_specs=[V, V, V],
        out_shape=[
            jax.ShapeDtypeStruct((groups * rows, 3 * width), bf16),
            jax.ShapeDtypeStruct((d, width), bf16),
            jax.ShapeDtypeStruct((groups, width - rows, width), bf16),
        ],
        scratch_shapes=[pltpu.VMEM((4, groups, width, width), bf16), pltpu.VMEM((width, d), bf16), pltpu.SemaphoreType.DMA((8 * groups,))],
        cost_estimate=kernel_cost(5.8),
        compiler_params=pltpu.CompilerParams(vmem_limit_bytes=VMEM_LIMIT),
        name="attention_weights",
    )(scal, *mine, *other)


def gradients_kernel(*refs):
    scal = refs[0]
    mine, other = refs[1:3]
    grads, (grad_out, small, buf, sems) = refs[3:6], refs[6:]
    rows = grads[0].shape[0]
    width = buf.shape[-1]
    half = width // 2
    out_rows, d = grad_out.shape
    copies = Copies(sems)
    done = []
    for j in range(4):
        for side, arrays in ((scal[2], mine), (1 - scal[2], other)):
            done.append(copies.start(arrays.at[j], buf.at[scal[1] ^ j, pl.ds(pl.multiple_of(side * half, 16), half)]))
    wait(done)
    for m in range(3):
        grads[m][...] = buf[m, :rows].astype(f32)
    for i in range(-(-d // width)):
        n = min(width, d - i * width)
        grad_out[:, i * width : i * width + n] = buf[3, i * out_rows : (i + 1) * out_rows, :n].astype(f32)
    small[...] = buf[0, rows:].astype(f32)


def attention_gradients(scal, mine, other, rows, out_rows, d):
    _, half, width = mine.shape
    V = pl.BlockSpec(memory_space=pltpu.VMEM)
    return pl.pallas_call(
        gradients_kernel,
        in_specs=[pl.BlockSpec(memory_space=pltpu.SMEM)] + [ANY] * 2,
        out_specs=[V] * 5,
        out_shape=[
            *[jax.ShapeDtypeStruct((rows, width), f32)] * 3,
            jax.ShapeDtypeStruct((out_rows, d), f32),
            jax.ShapeDtypeStruct((width - rows, width), f32),
        ],
        scratch_shapes=[pltpu.VMEM((4, width, width), bf16), pltpu.SemaphoreType.DMA((8,))],
        cost_estimate=kernel_cost(3.5),
        compiler_params=pltpu.CompilerParams(vmem_limit_bytes=VMEM_LIMIT),
        name="attention_gradients",
    )(scal, mine, other)


def down_kernel(*refs):
    scal = refs[0]
    mine, other = refs[1:3]
    out, buf, sems = refs[3:]
    half = buf.shape[0] // 8
    copies = Copies(sems)
    done = []
    for j in range(4):
        for side, arrays in ((scal[2], mine), (1 - scal[2], other)):
            at = ((scal[1] ^ j) * 2 + side) * half
            done.append(copies.start(arrays.at[j], buf.at[pl.ds(pl.multiple_of(at, 16), half)]))
    wait(done)
    for i in range(buf.shape[0] // 128):
        rows = slice(i * 128, (i + 1) * 128)
        out[:, rows] = buf[rows].astype(f32).T


def down_gradient(scal, mine, other):
    _, half, d = mine.shape
    return pl.pallas_call(
        down_kernel,
        in_specs=[pl.BlockSpec(memory_space=pltpu.SMEM)] + [ANY] * 2,
        out_specs=pl.BlockSpec(memory_space=pltpu.VMEM),
        out_shape=jax.ShapeDtypeStruct((d, 8 * half), f32),
        scratch_shapes=[pltpu.VMEM((8 * half, d), bf16), pltpu.SemaphoreType.DMA((8,))],
        cost_estimate=kernel_cost(5.6),
        compiler_params=pltpu.CompilerParams(vmem_limit_bytes=VMEM_LIMIT),
        name="down_gradient",
    )(scal, mine, other)


def dot(left, right, form):
    return jnp.einsum(form, left, right, preferred_element_type=f32)


def add(*terms):
    total = terms[0].astype(f32)
    for term in terms[1:]:
        total = total + term.astype(f32)
    return total.astype(bf16)


def after(v, *others):
    return lax.optimization_barrier((v, others))[0]


def tie(*values):
    return lax.optimization_barrier(values)


def pick(stack, i):
    return lax.dynamic_index_in_dim(stack, i, 0, keepdims=False)


SHARD = ("outer", "chip", "core")


class Links:
    def __init__(self, shards, groups):
        self.shards, self.groups = shards, groups
        self.z = lax.axis_index("group")
        self.index = lax.axis_index(SHARD)
        self.core = self.index & 1
        self.chip = (self.index >> 1) & 3

    def swap(self, v, bit):
        return lax.ppermute(v, SHARD, [(i, i ^ bit) for i in range(self.shards)])

    def turn(self, v, k):
        return lax.ppermute(v, "group", [(i, (i + k) % self.groups) for i in range(self.groups)])

    def ring_gather(self, v):
        return [v] + [self.turn(v, k) for k in range(1, self.groups)]

    def others(self, v):
        return jnp.stack([pick(v, (self.z - k) % self.groups) for k in range(1, self.groups)])

    def ring_reduce(self, v, *others):
        at = lambda k: pick(v, (self.z + k) % self.groups)
        total = at(0).astype(f32)
        for k in range(1, self.groups):
            total = total + after(self.turn(at(k), k), *others).astype(f32)
        return total

    def beyond(self, total):
        bit = 8
        while bit < self.shards:
            total = total + self.swap(total, bit)
            bit *= 2
        return total


def local(
    layer_input_rows,
    gain_attn,
    w_query,
    w_key,
    w_value,
    w_out,
    gain_ff,
    gate_weight,
    w_up,
    w_down,
    bucket_head_bias,
    positions,
    rel_bucket,
    out_grad,
    *,
    shards,
    groups,
):
    links = Links(shards, groups)
    z, core, chip = links.z, links.core, links.chip
    tokens, d = layer_input_rows.shape
    seqs = tokens // SEQ
    width = w_query.shape[1]
    rows = w_query.shape[0]
    buckets = bucket_head_bias.shape[0] * groups
    scals = [jnp.stack([z, chip ^ j, core]).astype(jnp.int32) for j in range(4)]
    scal = scals[0]

    small = jnp.concatenate([gain_attn, gain_ff, bucket_head_bias.reshape(-1)])
    spare = width - rows
    small = jnp.pad(small, (0, spare * width - small.shape[0])).reshape(spare, width)
    out_blocks = -(-d // width)
    wo_block = jnp.pad(w_out, ((0, 0), (0, out_blocks * width - d)))
    wo_block = jnp.concatenate([wo_block[:, i * width : (i + 1) * width] for i in range(out_blocks)])
    tall = lambda w: jnp.concatenate([w, small])
    four = jnp.stack([tall(w_query), tall(w_key), tall(w_value), wo_block])
    half = width // 2
    piece = lax.dynamic_slice(four, (chip, core * half, 0), (1, half, width))[0]
    slots = links.ring_gather(piece)
    own_gate, own_up = split_columns(gate_weight, w_up)
    slots[1:] = after(slots[1:], own_gate)
    mine = [jnp.stack(slots)]
    x_t, g_t = layer_input_rows.T, out_grad.T
    g = lax.optimization_barrier(out_grad)
    arrived = [links.swap(mine[0], bit) for bit in (XBIT, YBIT, XBIT | YBIT)]
    mine += [after(a, g) for a in arrived]
    wqkv, wo_t, smalls = attention_weights(scal, mine, [links.swap(a, CORE) for a in mine], rows, d)
    smalls = smalls.reshape(groups, -1)
    gains = [smalls[:, i * rows : (i + 1) * rows].reshape(d, 1).astype(f32) for i in range(2)]
    bias_table = smalls[:, 2 * rows : 2 * rows + bucket_head_bias.size].reshape(buckets, H)

    own_down = w_down.reshape(4, -1, d)
    half_down = own_down.shape[1] // 2
    whole = lambda v: lax.all_gather(v, ("core", "group")).reshape(2, groups, *v.shape)
    gate_up_of = lambda p: jnp.where(core == 0, pick(own_gate, p), pick(own_up, p))
    down_of = lambda p: lax.dynamic_slice(own_down, (p, core * half_down, 0), (1, half_down, d))[0]
    near_gu = whole(after(gate_up_of(chip), *slots[1:]))

    inputs = x_t.astype(f32)
    r_attn = lax.rsqrt(jnp.mean(inputs * inputs, axis=0, keepdims=True) + FLOOR)
    normed_t = (inputs * r_attn * gains[0]).astype(bf16)
    qkv = dot(normed_t, wqkv, "dt,dc->tc").astype(bf16)
    onehot = (rel_bucket[:, None] == jnp.arange(buckets, dtype=jnp.int32)[None, :]).astype(f32)
    offsets = jnp.dot(onehot, bias_table.astype(f32), precision=lax.Precision.HIGHEST).T
    bias = bias_matrix(offsets[:, None, :])
    near_dn = whole(after(down_of(chip), bias))
    places = (positions // BLOCK).reshape(seqs, SEQ)
    bias, near_gu = tie(bias, near_gu)
    gu = links.others(pick(near_gu, core))
    gu_x, gu_y = links.swap(gu, XBIT), links.swap(gu, YBIT)
    attend, context = attend_forward(qkv, bias, places[:, :, None], places[:, None, :])
    middle_t, normed_ff_t, normed_ff = middle_norm(context, wo_t, x_t, gains[1])
    normed_ff, gu_x, gu_y = tie(normed_ff, gu_x, gu_y)
    dn = links.others(pick(after(near_dn, context), core))
    dn_x, dn_y = links.swap(dn, XBIT), links.swap(dn, YBIT)
    far_gu = whole(after(gate_up_of(chip ^ 3), qkv))
    gus, dns = [near_gu], [near_dn]
    both = lambda parts: (parts, [links.swap(a, CORE) for a in parts])

    acts, sums_gu, sums_dn = [None] * 4, [None] * 4, [None] * 4

    def chunk(j, *deps):
        hid, dg, du, gm, go, dm, do = ffn_chunk(
            after(scals[j], *deps), normed_ff, normed_ff_t, g, own_gate, own_up, own_down, gus[j], dns[j]
        )
        acts[j] = (hid, dg, du)
        sums_gu[j] = add(gm, links.swap(go, CORE))
        sums_dn[j] = add(dm, links.swap(do, CORE))
        return hid

    scatter = lambda v: lax.psum_scatter(v, "group", scatter_dimension=0)
    done = chunk(0)
    gu_x, gu_y, dn_x, dn_y = after((gu_x, gu_y, dn_x, dn_y), done)
    gus += [both([gu_x]), both([gu_y])]
    dns += [both([dn_x]), both([dn_y])]
    far_dn = links.swap(after(dn, done), XBIT | YBIT)
    rings = [None] * 4
    rings[0] = scatter(sums_dn[0])
    done = chunk(1, done)
    done, far_dn, far_gu = tie(done, far_dn, far_gu)
    gus.append(far_gu)
    dns.append(both([far_dn]))
    done = chunk(2, done, sums_dn[0])
    rings[1] = scatter(sums_dn[1])
    done, rings[0] = tie(done, rings[0])
    done = chunk(3, done, sums_gu[0], sums_gu[1], sums_dn[1])
    done, rings[1] = tie(done, rings[1])
    from_x, from_y = links.swap(sums_gu[1], XBIT), links.swap(sums_gu[2], YBIT)
    pair = scatter(jnp.stack([sums_dn[2], sums_dn[3]], axis=1))
    rings[2:] = pair[0], pair[1]
    far_sum = scatter(sums_gu[3].reshape(groups, rows, -1))
    d_middle_t, d_attn_t, grad_gain_ff = ffn_dx(
        after(scal, done, sums_gu[2], sums_gu[3], sums_dn[2], sums_dn[3]),
        gains[1],
        middle_t,
        g_t,
        own_gate,
        own_up,
        [(acts[j][1], acts[j][2], gus[j]) for j in range(4)],
    )
    d_context = dot(d_attn_t, wo_t, "dt,dc->tc").astype(bf16)
    d_context, from_x, from_y, *rings = tie(d_context, from_x, from_y, *rings)
    d_q, d_k, d_v, per_offset = attend_backward(qkv, attend, d_context)
    far = after([links.swap(rings[j], j << 1) for j in (1, 2, 3)], d_q)
    red_dn = rings[0].astype(f32)
    for part in far:
        red_dn = red_dn + part.astype(f32)
    red_dn = links.beyond(red_dn).astype(bf16)
    red_gu = scatter(add(sums_gu[0], from_x, from_y).reshape(groups, rows, -1))
    d_q, red_dn = tie(d_q, red_dn)
    grad_table = jnp.dot(onehot.T, per_offset[:, 0, :].T, precision=lax.Precision.HIGHEST)
    input_grad_t, grad_gain_attn = input_gradient(d_q, d_k, d_v, wqkv, x_t, d_middle_t, gains[0])

    def spread(v, *others):
        received = [after(links.swap(v, j << 1), *others) for j in (1, 2, 3)]
        mine = jnp.stack([v, *received])
        return mine, links.swap(mine, CORE)

    received = [links.swap(red_dn, j << 1) for j in (1, 2, 3)]
    input_grad_t, far_sum, *received = tie(input_grad_t, far_sum, *received)
    dn_mine = jnp.stack([red_dn, *received])
    dn_other = links.swap(dn_mine, CORE)
    far_sum = links.swap(far_sum, XBIT | YBIT)

    small = [grad_gain_attn.reshape(groups, -1), grad_gain_ff.reshape(groups, -1), grad_table.reshape(groups, -1)]
    small = jnp.concatenate(small, axis=1).astype(bf16)
    small = jnp.pad(small, ((0, 0), (0, spare * width - small.shape[1]))).reshape(groups, spare, width)
    mine, other = attention_matrices(after(scal, input_grad_t), normed_t, d_q, d_k, d_v, context, d_attn_t, small)
    mine, dn_other = tie(mine, dn_other)
    sums = add(mine, links.swap(other, CORE))
    output_t = ffn_out(after(scal, sums), middle_t, own_down, [(acts[j][0], dns[j]) for j in range(4)])
    plane = [links.swap(pick(sums, chip ^ j), j << 1) for j in (1, 2, 3)]
    output_t, far_sum, red_gu, *plane = tie(output_t, far_sum, red_gu, *plane)
    red_plane = add(pick(sums, chip), *plane)
    red_gu = links.beyond(red_gu.astype(f32) + far_sum.astype(f32)).astype(bf16)
    red_gu, red_plane = tie(red_gu, red_plane)
    red = scatter(red_plane)
    gu_x, gu_y = links.swap(red_gu, XBIT), links.swap(red_gu, YBIT)
    grad_down = down_gradient(scal, dn_mine, after(dn_other, red_gu)).T
    gu_x, gu_y, red, grad_down = tie(gu_x, gu_y, red, grad_down)
    mid = rows // 2
    gu_d = jnp.concatenate([links.swap(gu_x[:mid], YBIT), links.swap(gu_y[mid:], XBIT)])
    spread_gu = jnp.stack([red_gu, gu_x, gu_y, gu_d])
    grad_gate, grad_up = join_columns(scal, spread_gu, links.swap(spread_gu, CORE))
    *wide, grad_out, small = attention_gradients(scal, *spread(links.beyond(red.astype(f32)).astype(bf16)), rows, *w_out.shape)
    small = small.reshape(-1)
    return (
        output_t.T,
        input_grad_t.T,
        small[:rows],
        wide[0],
        wide[1],
        wide[2],
        grad_out,
        small[rows : 2 * rows],
        grad_gate,
        grad_up,
        grad_down,
        small[2 * rows : 2 * rows + bucket_head_bias.size].reshape(bucket_head_bias.shape),
    )


def solution(mesh):
    shards, groups = mesh.shape["shard"], mesh.shape["group"]
    mesh = jax.sharding.Mesh(mesh.devices.reshape(shards // 8, 4, 2, groups), (*SHARD, "group"))
    split = P((*SHARD, "group"), None)
    rows = P("group", None)
    in_specs = (split, P("group"), rows, rows, rows, rows, P("group"), rows, rows, rows, rows, P((*SHARD, "group")), P(), split)
    out_specs = (split, split, P("group"), rows, rows, rows, rows, P("group"), rows, rows, rows, rows)
    body = functools.partial(local, shards=shards, groups=groups)
    return jax.shard_map(body, mesh=mesh, in_specs=in_specs, out_specs=out_specs, check_vma=False)
```
